32 devices in a mesh: ha: 2 (over y), wa: 4 (over z), hd: 4 (over x, core).
Axes of the slice: x: 2, y: 2, z: 4, core: 2. Of those that a mesh axis runs over, the one named last changes fastest.
Arguments:
- q_raw: bfloat16 [2, 4, 128, 2560], P('ha', 'wa', None, 'hd')
- k_raw: bfloat16 [2, 4, 128, 2560], P('ha', 'wa', None, 'hd')
- values: bfloat16 [2, 4, 128, 2560], P('ha', 'wa', None, 'hd')
- upstream: bfloat16 [2, 4, 128, 2560], P('ha', 'wa', None, 'hd'), may hold values from -384 to 384
- outputs: bfloat16 [2, 4, 128, 2560], P('ha', 'wa', None, 'hd')
- logsumexp: float32 [2, 4, 20, 128], P('ha', 'wa', 'hd'), may hold values from 7.5 to 9.5
- gain_q: bfloat16 [2560], P('hd'), may hold values from 0.25 to 1.75
- gain_k: bfloat16 [2560], P('hd'), may hold values from 0.25 to 1.75
- far_list: int32 [2, 4, 12], P('ha'), may hold values from -1 to 15, as said below
Outputs:
- dq_raw: bfloat16 [2, 4, 128, 2560], P('ha', 'wa', None, 'hd')
- dk_raw: bfloat16 [2, 4, 128, 2560], P('ha', 'wa', None, 'hd')
- dv: bfloat16 [2, 4, 128, 2560], P('ha', 'wa', None, 'hd')
The draws below stay inside these ranges and needn't reach their ends.
Inputs may be any that keep to these rules, and one draw needn't show every extreme that they name: far_list[r, c, f] is -1 (an empty slot) or names key unit u of tile (r, u // 4); the named tiles lie two or more columns away from c, and each is named at most once in far_list[r, c].
All inputs are finite; a program needn't handle non-finite values.
Results may differ from the reference program's by a relative error of at most 0.0015.
The reference program's roundings to bfloat16 on the way (of `dscore`, `weight_low`, `dq_norm` and `dk_norm`) count: a program that leaves them out, or rounds other values in their place, can miss the bound.
Values may be sent and summed in bfloat16 or wider, within the bound.
A program may use at most 64 MiB of HBM per device.

```python
import math
import jax
import jax.numpy as jnp
from jax import lax

HEADS = 20
HEAD = 128
TOK_DEV = 128
UNITS = 4
FAR = 12
TROWS = 2
TCOLS = 4
HW = 2560
KB = 32


def ramp_draw(key):
    shape = (TROWS, TCOLS, TOK_DEV, HW)
    head_place = (jnp.arange(HW) // HEAD).astype(jnp.float32) / max(HEADS - 1, 1)
    parts = jax.random.split(key, 1)
    base = jax.random.normal(parts[0], shape, jnp.float32)
    ramp = jnp.exp(0.5 * math.log(3.0) * head_place)
    return (base * ramp).astype(jnp.bfloat16)


def draw_q_raw(key, part):
    return ramp_draw(jax.random.fold_in(key, 101))


def draw_k_raw(key, part):
    return ramp_draw(jax.random.fold_in(key, 202))


def channel_mean(key):
    return jax.random.normal(jax.random.fold_in(key, 303), (HW,), jnp.float32)


def noise_draw(key):
    shape = (TROWS, TCOLS, TOK_DEV, HW)
    return jax.random.normal(key, shape, jnp.float32)


def draw_values(key, part):
    return (channel_mean(key) + noise_draw(jax.random.fold_in(key, 404))).astype(jnp.bfloat16)


def draw_outputs(key, part):
    return (channel_mean(key) + 0.15 * noise_draw(jax.random.fold_in(key, 505))).astype(jnp.bfloat16)


def draw_far_list(key, part):
    parts = jax.random.split(jax.random.fold_in(key, 606), 4)
    owners = jnp.arange(TCOLS, dtype=jnp.int32)
    column = owners[None, :, None]
    peer = owners[None, None, :]
    popularity = jax.random.randint(parts[0], (TROWS, 1, TCOLS), 0, TCOLS)
    jitter = jax.random.randint(parts[1], (TROWS, TCOLS, TCOLS), 0, TCOLS)
    score = 2 * popularity + jitter
    eligible = jnp.abs(peer - column) >= 2
    score = jnp.where(eligible, score, 4 * TCOLS)
    forced = (column == 0) & (peer == TCOLS - 1)
    score = jnp.where(forced, -1, score)
    ranked = jnp.argsort(score * TCOLS + peer, axis=-1, stable=True).astype(jnp.int32)
    filler = jnp.zeros((TROWS, TCOLS, FAR), jnp.int32)
    ranked = jnp.concatenate([ranked, filler], axis=-1)[..., :FAR]
    available = jnp.broadcast_to(jnp.sum(eligible, axis=-1).astype(jnp.int32), (TROWS, TCOLS))
    wanted = jax.random.randint(parts[2], (TROWS, TCOLS), max(FAR - 2, 1), FAR + 1)
    wanted = jnp.where(owners[None, :] == 1, max(FAR - 2, 1), wanted)
    count = jnp.minimum(wanted, available)
    slot = jnp.arange(FAR, dtype=jnp.int32)
    unit = jax.random.randint(parts[3], (TROWS, TCOLS, FAR), 0, UNITS)
    unit = jnp.where((owners[None, :, None] == 0) & (slot[None, None, :] == 0), UNITS - 1, unit)
    return jnp.where(slot[None, None, :] < count[..., None], ranked * UNITS + unit, -1).astype(jnp.int32)


def shard_levels(own_key, extent, pieces, smallest, high):
    def one(position, blocks):
        draws = jax.random.uniform(jax.random.fold_in(jax.random.fold_in(own_key, 6), position), (blocks,), jnp.float32, smallest / len(pieces), high / len(pieces))
        return jnp.repeat(jnp.exp(draws), extent[position] // blocks).reshape((-1,) + (1,) * (len(extent) - position - 1))

    loudness = one(*pieces[0])
    for cut in pieces[1:]:
        loudness = loudness * one(*cut)
    return loudness


def bell_draw(key, extent, deviation, most, pieces=(), kind=jnp.bfloat16):
    result = jax.random.normal(key, extent, jnp.float32) * deviation
    if len(pieces) > 0:
        result = shard_levels(key, extent, pieces, -0.22, 0.18) * result
    return jnp.clip(result, min=-most, max=most).astype(kind)


def setup_inputs(seed: int = 0) -> dict:
    streams_of = jax.random.split(jax.random.key(seed), 10)
    return {
        "q_raw": draw_q_raw(jax.random.fold_in(streams_of[9], 71), 0),
        "k_raw": draw_k_raw(jax.random.fold_in(streams_of[9], 71), 0),
        "values": draw_values(jax.random.fold_in(streams_of[9], 71), 0),
        "upstream": bell_draw(streams_of[3], (TROWS, TCOLS, TOK_DEV, HW), 64.0, 384.0, ((0, 2), (1, 4), (3, 4))),
        "outputs": draw_outputs(jax.random.fold_in(streams_of[9], 71), 0),
        "logsumexp": jnp.clip(7.5 + 2.0 * jax.random.uniform(streams_of[5], (TROWS, TCOLS, HEADS, TOK_DEV), jnp.float32) ** shard_levels(streams_of[5], (TROWS, TCOLS, HEADS, TOK_DEV), ((0, 2), (1, 4), (2, 4)), -0.2, 0.2), 7.5, 9.5),
        "gain_q": jnp.clip(1.0 + 0.15 * jax.random.normal(streams_of[6], (HW,), jnp.float32), 0.25, 1.75).astype(jnp.bfloat16),
        "gain_k": jnp.clip(1.0 + 0.15 * jax.random.normal(streams_of[7], (HW,), jnp.float32), 0.25, 1.75).astype(jnp.bfloat16),
        "far_list": draw_far_list(jax.random.fold_in(streams_of[9], 71), 0),
    }


EPS = 1e-06
POSITIONS = ((1, 1), (0, 1), (2, 1), (1, 0), (1, 2))

def rounded(array):
    return lax.optimization_barrier(array.astype(jnp.bfloat16)).astype(jnp.float32)

def norm_rows(raw, gain):
    raw_wide = raw.astype(jnp.float32)
    rate = lax.rsqrt(lax.optimization_barrier(jnp.mean(raw_wide * raw_wide, axis=-1)) + EPS)
    return ((raw_wide * rate[..., None] * gain.astype(jnp.float32)).astype(jnp.bfloat16), rate)

def block_terms(queries, upstream_tile, lse_tile, delta_tile, keys, vals, key_valid):
    query_count = queries.shape[0]
    key_count = keys.shape[0]
    query_heads = queries.astype(jnp.float32).reshape(query_count, HEADS, HEAD)
    upstream_heads = upstream_tile.astype(jnp.float32).reshape(query_count, HEADS, HEAD)
    key_heads = keys.astype(jnp.float32).reshape(key_count, HEADS, HEAD)
    value_heads = vals.astype(jnp.float32).reshape(key_count, HEADS, HEAD)
    scores = jnp.einsum('ihd,jhd->hij', query_heads, key_heads) / math.sqrt(HEAD)
    weight = jnp.where(key_valid[None, None, :], jnp.exp(scores - lse_tile[:, :, None]), 0.0)
    dweight = jnp.einsum('ihd,jhd->hij', upstream_heads, value_heads)
    dscore = rounded(weight * (dweight - delta_tile[:, :, None]))
    weight_low = rounded(weight)
    return (query_heads, upstream_heads, key_heads, dscore, weight_low)

def query_side(queries, upstream_tile, lse_tile, delta_tile, keys, vals, key_valid):
    query_heads, upstream_heads, key_heads, dscore, weight_low = block_terms(queries, upstream_tile, lse_tile, delta_tile, keys, vals, key_valid)
    grads = jnp.einsum('hij,jhd->ihd', dscore, key_heads) / math.sqrt(HEAD)
    return grads.reshape(queries.shape[0], HW).astype(jnp.bfloat16)

def key_side(queries, upstream_tile, lse_tile, delta_tile, keys, vals, key_valid):
    query_heads, upstream_heads, key_heads, dscore, weight_low = block_terms(queries, upstream_tile, lse_tile, delta_tile, keys, vals, key_valid)
    key_grads = jnp.einsum('hij,ihd->jhd', dscore, query_heads) / math.sqrt(HEAD)
    value_grads = jnp.einsum('hij,ihd->jhd', weight_low, upstream_heads)
    count = keys.shape[0]
    return (key_grads.reshape(count, HW).astype(jnp.bfloat16), value_grads.reshape(count, HW).astype(jnp.bfloat16))

def pick(array, row, col):
    inner = lax.dynamic_index_in_dim(array, row, 0, keepdims=False)
    return lax.dynamic_index_in_dim(inner, col, 0, keepdims=False)

def tile_exists(row, col):
    return (row >= 0) & (row < TROWS) & (col >= 0) & (col < TCOLS)

def reference(q_raw, k_raw, values, upstream, outputs, logsumexp, gain_q, gain_k, far_list):
    query_norm, q_rate = norm_rows(q_raw, gain_q)
    key_norm, k_rate = norm_rows(k_raw, gain_k)
    product = upstream.astype(jnp.float32) * outputs.astype(jnp.float32)
    delta = lax.optimization_barrier(jnp.sum(product.reshape(TROWS, TCOLS, TOK_DEV, HEADS, HEAD), axis=-1)).transpose(0, 1, 3, 2)
    padding = ((1, 1), (1, 1), (0, 0), (0, 0))
    key_pad = jnp.pad(key_norm, padding)
    value_pad = jnp.pad(values, padding)
    query_pad = jnp.pad(query_norm, padding)
    upstream_pad = jnp.pad(upstream, padding)
    lse_pad = jnp.pad(logsumexp, padding)
    delta_pad = jnp.pad(delta, padding)

    def query_tile(flat):
        row = (flat // TCOLS).astype(jnp.int32)
        col = (flat % TCOLS).astype(jnp.int32)
        win_keys = jnp.concatenate([pick(key_pad, row + row_step, col + col_step) for row_step, col_step in POSITIONS], 0)
        win_vals = jnp.concatenate([pick(value_pad, row + row_step, col + col_step) for row_step, col_step in POSITIONS], 0)
        win_valid = jnp.concatenate([jnp.broadcast_to(tile_exists(row + row_step - 1, col + col_step - 1), (TOK_DEV,)) for row_step, col_step in POSITIONS], 0)
        listed = pick(far_list, row, col)
        safe = jnp.maximum(listed, 0)
        owner = (safe // UNITS).astype(jnp.int32)
        first = (safe % UNITS * KB).astype(jnp.int32)

        def one_unit(owner_col, start):
            unit_keys = lax.dynamic_slice_in_dim(pick(key_norm, row, owner_col), start, KB, 0)
            unit_vals = lax.dynamic_slice_in_dim(pick(values, row, owner_col), start, KB, 0)
            return (unit_keys, unit_vals)
        far_keys, far_vals = jax.vmap(one_unit)(owner, first)
        keys = jnp.concatenate([win_keys, far_keys.reshape(FAR * KB, HW)], 0)
        vals = jnp.concatenate([win_vals, far_vals.reshape(FAR * KB, HW)], 0)
        valid = jnp.concatenate([win_valid, jnp.repeat(listed >= 0, KB)], 0)
        return query_side(pick(query_norm, row, col), pick(upstream, row, col), pick(logsumexp, row, col), pick(delta, row, col), keys, vals, valid)
    tiles = jnp.arange(TROWS * TCOLS, dtype=jnp.int32)
    dq_norm = lax.map(query_tile, tiles).reshape(TROWS, TCOLS, TOK_DEV, HW)

    def key_tile(flat):
        row = (flat // TCOLS).astype(jnp.int32)
        col = (flat % TCOLS).astype(jnp.int32)
        own_keys = pick(key_norm, row, col)
        own_vals = pick(values, row, col)
        total_key = jnp.zeros((TOK_DEV, HW), jnp.float32)
        total_value = jnp.zeros((TOK_DEV, HW), jnp.float32)
        for row_step, col_step in POSITIONS:
            valid = jnp.broadcast_to(tile_exists(row + row_step - 1, col + col_step - 1), (TOK_DEV,))
            part_key, part_value = key_side(pick(query_pad, row + row_step, col + col_step), pick(upstream_pad, row + row_step, col + col_step), pick(lse_pad, row + row_step, col + col_step), pick(delta_pad, row + row_step, col + col_step), own_keys, own_vals, valid)
            total_key = total_key + part_key.astype(jnp.float32)
            total_value = total_value + part_value.astype(jnp.float32)

        def add_far(source, carry):
            sum_key, sum_value = carry
            source = jnp.asarray(source).astype(jnp.int32)
            listed = pick(far_list, row, source)
            asked = (listed >= 0) & (listed // UNITS == col)
            present = jnp.any(asked)
            unit = jnp.sum(jnp.where(asked, listed % UNITS, 0)).astype(jnp.int32)
            unit_keys = lax.dynamic_slice_in_dim(own_keys, unit * KB, KB, 0)
            unit_vals = lax.dynamic_slice_in_dim(own_vals, unit * KB, KB, 0)
            part_key, part_value = key_side(pick(query_norm, row, source), pick(upstream, row, source), pick(logsumexp, row, source), pick(delta, row, source), unit_keys, unit_vals, jnp.broadcast_to(present, (KB,)))
            place = (jnp.arange(UNITS, dtype=jnp.int32) == unit).astype(jnp.float32)
            sum_key = sum_key + place[:, None, None] * part_key.astype(jnp.float32)[None]
            sum_value = sum_value + place[:, None, None] * part_value.astype(jnp.float32)[None]
            return (sum_key, sum_value)
        empty = jnp.zeros((UNITS, KB, HW), jnp.float32)
        far_key, far_value = lax.fori_loop(0, TCOLS, add_far, (empty, empty))
        key_grad = (total_key + far_key.reshape(TOK_DEV, HW)).astype(jnp.bfloat16)
        value_grad = (total_value + far_value.reshape(TOK_DEV, HW)).astype(jnp.bfloat16)
        return (key_grad, value_grad)
    dk_norm, dv = lax.map(key_tile, tiles)
    dk_norm = dk_norm.reshape(TROWS, TCOLS, TOK_DEV, HW)
    dv = dv.reshape(TROWS, TCOLS, TOK_DEV, HW)
    gain_qw = gain_q.astype(jnp.float32)
    gain_kw = gain_k.astype(jnp.float32)
    q_wide = q_raw.astype(jnp.float32)
    k_wide = k_raw.astype(jnp.float32)
    dq_wide = dq_norm.astype(jnp.float32)
    dk_wide = dk_norm.astype(jnp.float32)
    q_dot = lax.optimization_barrier(jnp.sum(gain_qw * dq_wide * q_wide, axis=-1))
    k_dot = lax.optimization_barrier(jnp.sum(gain_kw * dk_wide * k_wide, axis=-1))
    dq_raw = (q_rate[..., None] * gain_qw * dq_wide - q_wide * (q_rate ** 3 * q_dot / HW)[..., None]).astype(jnp.bfloat16)
    dk_raw = (k_rate[..., None] * gain_kw * dk_wide - k_wide * (k_rate ** 3 * k_dot / HW)[..., None]).astype(jnp.bfloat16)
    return (dq_raw, dk_raw, dv)
```

```python
import functools
import math

import jax
import jax.numpy as jnp
from jax import lax
from jax.experimental import pallas as pl
from jax.experimental.pallas import tpu as pltpu
from jax.sharding import PartitionSpec as P

UNITS = 4
EPS = 1e-06
MESH = pl.DeviceIdType.MESH
LAST = (((1,), (1,)), ((), ()))
FIRST = (((0,), (0,)), ((), ()))
PLAIN = (((1,), (0,)), ((), ()))
UP, DOWN, LEFT, RIGHT = range(4)
F32 = jnp.float32
BF16 = jnp.bfloat16


def dot(a, b, dims):
    return lax.dot_general(a, b, dims, preferred_element_type=F32)


def kernel(
    sizes,
    q_hbm,
    k_hbm,
    v_hbm,
    u_hbm,
    o_hbm,
    lse_ref,
    gain_q_ref,
    gain_k_ref,
    far_ref,
    dq_out,
    dk_out,
    dv_out,
    q_raw,
    k_raw,
    vals,
    ups,
    outs,
    qn,
    kn,
    delta_ref,
    dq_acc,
    own,
    halo,
    far_pack,
    far_in,
    ret_out,
    ret_in,
    fret_out,
    fret_in,
    total,
    xbuf,
    load_sem,
    halo_send,
    halo_recv,
    far_send,
    far_recv,
    ret_send,
    ret_recv,
    fret_send,
    fret_recv,
    x_send,
    x_recv,
):
    rows, cols, parts = sizes
    row = lax.axis_index("ha")
    col = lax.axis_index("wa")
    me = lax.axis_index("hd")
    tokens, width = q_raw.shape
    heads = lse_ref.shape[2]
    hw = width // heads
    kb = tokens // UNITS
    full_width = width * parts
    slots = far_ref.shape[2]
    score_scale = 1.0 / math.sqrt(hw)

    loads = []
    for index, (source, target) in enumerate(
        ((k_hbm, k_raw), (q_hbm, q_raw), (v_hbm, vals), (u_hbm, ups), (o_hbm, outs))
    ):
        copy = pltpu.make_async_copy(source.at[0, 0], target, load_sem.at[index])
        copy.start()
        loads.append(copy)

    exists = (row > 0, row < rows - 1, col > 0, col < cols - 1)
    ids = ({"ha": row - 1}, {"ha": row + 1}, {"wa": col - 1}, {"wa": col + 1})
    is_far = [(col - peer) * (col - peer) >= 4 for peer in range(cols)]

    barrier = pltpu.get_barrier_semaphore()
    hd_ids = [{"hd": lax.rem(me + off, parts)} for off in range(1, parts)]
    for target in hd_ids:
        pl.semaphore_signal(barrier, inc=1, device_id=target, device_id_type=MESH)
    for side in range(4):

        @pl.when(exists[side])
        def _(side=side):
            pl.semaphore_signal(barrier, inc=1, device_id=ids[side], device_id_type=MESH)

    for peer in range(cols):

        @pl.when(is_far[peer])
        def _(peer=peer):
            pl.semaphore_signal(barrier, inc=1, device_id={"wa": peer}, device_id_type=MESH)

    def lane_columns(columns):
        lane = lax.broadcasted_iota(jnp.int32, (tokens, 128), 1)
        mat = jnp.zeros((tokens, 128), F32)
        for place, column in columns:
            mat = jnp.where(lane == place, column, mat)
        return mat.T

    def row_sums(block):
        acc = block[:, :hw]
        for head in range(1, heads):
            acc = acc + block[:, head * hw : (head + 1) * hw]
        return jnp.sum(acc, axis=1, keepdims=True)

    def to_columns(rows8):
        return jnp.concatenate([rows8] * (tokens // 8), axis=0).T

    def x_copy(which, off):
        return pltpu.make_async_remote_copy(
            src_ref=xbuf.at[which, me],
            dst_ref=xbuf.at[which, me],
            send_sem=x_send.at[which, off],
            recv_sem=x_recv.at[which, off],
            device_id=hd_ids[off - 1],
            device_id_type=MESH,
        )

    def x_start(which, rows8):
        xbuf[which, me] = rows8
        for off in range(1, parts):
            x_copy(which, off).start()

    def x_finish(which):
        for off in range(1, parts):
            x_copy(which, off).wait()
        acc = xbuf[which, 0]
        for part in range(1, parts):
            acc = acc + xbuf[which, part]
        return acc

    def halo_copy(side, which, source):
        return pltpu.make_async_remote_copy(
            src_ref=source,
            dst_ref=halo.at[side ^ 1, which],
            send_sem=halo_send.at[side, which],
            recv_sem=halo_recv.at[side ^ 1, which],
            device_id=ids[side],
            device_id_type=MESH,
        )

    def halo_wait(side, which):
        pltpu.make_async_remote_copy(
            src_ref=vals,
            dst_ref=halo.at[side, which],
            send_sem=halo_send.at[side, which],
            recv_sem=halo_recv.at[side, which],
            device_id=ids[side],
            device_id_type=MESH,
        ).wait_recv()

    def far_copy(peer):
        return pltpu.make_async_remote_copy(
            src_ref=far_pack.at[peer],
            dst_ref=far_in.at[col],
            send_sem=far_send.at[peer],
            recv_sem=far_recv.at[col],
            device_id={"wa": peer},
            device_id_type=MESH,
        )

    def far_wait(peer):
        pltpu.make_async_remote_copy(
            src_ref=far_pack.at[peer],
            dst_ref=far_in.at[peer],
            send_sem=far_send.at[peer],
            recv_sem=far_recv.at[peer],
            device_id={"wa": peer},
            device_id_type=MESH,
        ).wait_recv()

    def ret_copy(side):
        return pltpu.make_async_remote_copy(
            src_ref=ret_out.at[side],
            dst_ref=ret_in.at[side ^ 1],
            send_sem=ret_send.at[side],
            recv_sem=ret_recv.at[side ^ 1],
            device_id=ids[side],
            device_id_type=MESH,
        )

    def ret_wait(side):
        pltpu.make_async_remote_copy(
            src_ref=ret_out.at[side],
            dst_ref=ret_in.at[side],
            send_sem=ret_send.at[side],
            recv_sem=ret_recv.at[side],
            device_id=ids[side],
            device_id_type=MESH,
        ).wait_recv()

    def fret_copy(peer):
        return pltpu.make_async_remote_copy(
            src_ref=fret_out.at[peer],
            dst_ref=fret_in.at[col],
            send_sem=fret_send.at[peer],
            recv_sem=fret_recv.at[col],
            device_id={"wa": peer},
            device_id_type=MESH,
        )

    def fret_wait(peer):
        pltpu.make_async_remote_copy(
            src_ref=fret_out.at[peer],
            dst_ref=fret_in.at[peer],
            send_sem=fret_send.at[peer],
            recv_sem=fret_recv.at[peer],
            device_id={"wa": peer},
            device_id_type=MESH,
        ).wait_recv()

    loads[0].wait()
    key_wide = k_raw[...].astype(F32)
    key_squares = row_sums(key_wide * key_wide)
    loads[1].wait()
    query_wide = q_raw[...].astype(F32)
    query_squares = row_sums(query_wide * query_wide)
    sums = lane_columns([(0, query_squares), (1, key_squares)])[0:8]
    loads[2].wait()

    pl.semaphore_wait(
        barrier,
        parts
        - 1
        + jnp.minimum(row, 1)
        + jnp.minimum(rows - 1 - row, 1)
        + (cols - 1),
    )
    x_start(0, sums)
    for side in range(4):

        @pl.when(exists[side])
        def _(side=side):
            halo_copy(side, 1, vals).start()

    loads[3].wait()
    loads[4].wait()
    delta_columns = []
    for head in range(heads):
        lanes = slice(head * hw, (head + 1) * hw)
        product = ups[:, lanes].astype(F32) * outs[:, lanes].astype(F32)
        delta_columns.append((head, jnp.sum(product, axis=1, keepdims=True)))
    delta_ref[...] = lane_columns(delta_columns)[0 : delta_ref.shape[0]]

    mine_used = []
    send_unit = []
    send_used = []
    for peer in range(cols):
        used = jnp.int32(0)
        unit = jnp.int32(0)
        asked = jnp.int32(0)
        for slot in range(slots):
            named = far_ref[0, col, slot] - peer * UNITS
            used = jnp.where((named >= 0) & (named < UNITS), 1, used)
            wanted = far_ref[0, peer, slot] - col * UNITS
            hit = (wanted >= 0) & (wanted < UNITS)
            unit = jnp.where(hit, wanted, unit)
            asked = jnp.where(hit, 1, asked)
        mine_used.append(used)
        send_unit.append(unit)
        send_used.append(asked)

    def pick_unit(peer, source):
        wanted = jnp.full((kb, width), send_unit[peer], jnp.int32)
        picked = source[0:kb, :].astype(F32)
        for unit in range(1, UNITS):
            block = source[unit * kb : (unit + 1) * kb, :].astype(F32)
            picked = jnp.where(wanted == unit, block, picked)
        return picked.astype(BF16)

    for peer in range(cols):

        @pl.when(is_far[peer])
        def _(peer=peer):
            far_pack[peer, 1] = pick_unit(peer, vals)

        @pl.when(jnp.logical_not(is_far[peer]))
        def _(peer=peer):
            far_in[peer] = jnp.zeros(far_in.shape[1:], BF16)

    gain_q = gain_q_ref[...].astype(F32)
    gain_k = gain_k_ref[...].astype(F32)
    rates = lax.rsqrt(x_finish(0) / full_width + EPS)
    rate_columns = to_columns(rates)
    q_rate = rate_columns[:, 0:1]
    k_rate = rate_columns[:, 1:2]
    kn[...] = (k_raw[...].astype(F32) * k_rate * gain_k).astype(BF16)
    for side in range(4):

        @pl.when(exists[side])
        def _(side=side):
            halo_copy(side, 0, kn).start()

    for peer in range(cols):

        @pl.when(is_far[peer])
        def _(peer=peer):
            far_pack[peer, 0] = pick_unit(peer, kn)
            far_copy(peer).start()

    qn[...] = (q_raw[...].astype(F32) * q_rate * gain_q).astype(BF16)

    def attend(head, key_head, value_head, mask):
        lanes = slice(head * hw, (head + 1) * hw)
        query_head = qn[:, lanes]
        upstream_head = ups[:, lanes]
        scores = dot(key_head, query_head, LAST) * score_scale
        weight = jnp.exp(scores - lse_ref[0, 0, head : head + 1, :])
        if mask is not None:
            weight = jnp.where(mask, weight, 0.0)
        dweight = dot(value_head, upstream_head, LAST)
        dscore = (weight * (dweight - delta_ref[head : head + 1, :])).astype(BF16)
        dq_part = dot(dscore, key_head, FIRST)
        dk_part = (dot(dscore, query_head, PLAIN) * score_scale).astype(BF16)
        dv_part = dot(weight.astype(BF16), upstream_head, PLAIN).astype(BF16)
        return dq_part, dk_part, dv_part

    for head in range(heads):
        lanes = slice(head * hw, (head + 1) * hw)
        dq_part, dk_part, dv_part = attend(head, kn[:, lanes], vals[:, lanes], None)
        dq_acc[:, lanes] = dq_part
        total[0, :, lanes] = dk_part.astype(F32)
        total[1, :, lanes] = dv_part.astype(F32)

    for side in range(4):

        @pl.when(exists[side])
        def _(side=side):
            halo_wait(side, 1)
            halo_wait(side, 0)
            for head in range(heads):
                lanes = slice(head * hw, (head + 1) * hw)
                dq_part, dk_part, dv_part = attend(
                    head, halo[side, 0, :, lanes], halo[side, 1, :, lanes], None
                )
                dq_acc[:, lanes] += dq_part
                ret_out[side, 0, :, lanes] = dk_part
                ret_out[side, 1, :, lanes] = dv_part
            ret_copy(side).start()

    for peer in range(cols):

        @pl.when(is_far[peer])
        def _(peer=peer):
            far_wait(peer)

    mask = jnp.concatenate(
        [jnp.full((kb, tokens), used, jnp.int32) for used in mine_used], axis=0
    ) > 0
    for head in range(heads):
        lanes = slice(head * hw, (head + 1) * hw)
        dq_part, dk_part, dv_part = attend(
            head,
            far_in[:, 0, :, lanes].reshape(cols * kb, hw),
            far_in[:, 1, :, lanes].reshape(cols * kb, hw),
            mask,
        )
        dq_acc[:, lanes] += dq_part
        fret_out[:, 0, :, lanes] = dk_part.reshape(cols, kb, hw)
        fret_out[:, 1, :, lanes] = dv_part.reshape(cols, kb, hw)
    for peer in range(cols):

        @pl.when(is_far[peer])
        def _(peer=peer):
            fret_copy(peer).start()

    dq_norm = (dq_acc[...] * score_scale).astype(BF16).astype(F32)
    query_wide = q_raw[...].astype(F32)
    weighted = gain_q * dq_norm
    x_start(1, lane_columns([(0, row_sums(weighted * query_wide))])[0:8])
    q_factor = rates * rates * rates * x_finish(1) / full_width
    q_factor = to_columns(q_factor)[:, 0:1]
    dq_out[0, 0] = (q_rate * weighted - query_wide * q_factor).astype(BF16)

    for side in range(4):

        @pl.when(exists[side])
        def _(side=side):
            ret_wait(side)
            total[...] += ret_in[side].astype(F32)

    for peer in range(cols):

        @pl.when(is_far[peer])
        def _(peer=peer):
            fret_wait(peer)
            for unit in range(UNITS):
                picked = jnp.where(send_unit[peer] == unit, send_used[peer], 0)
                spread = jnp.full((kb, width), picked, jnp.int32) > 0
                place = slice(unit * kb, (unit + 1) * kb)
                for which in range(2):
                    total[which, place, :] += jnp.where(
                        spread, fret_in[peer, which].astype(F32), 0.0
                    )

    dk_norm = total[0].astype(BF16).astype(F32)
    key_wide = k_raw[...].astype(F32)
    weighted = gain_k * dk_norm
    x_start(2, lane_columns([(1, row_sums(weighted * key_wide))])[0:8])
    dv_out[0, 0] = total[1].astype(BF16)
    for side in range(4):

        @pl.when(exists[side])
        def _(side=side):
            halo_copy(side, 1, vals).wait_send()
            halo_copy(side, 0, kn).wait_send()
            ret_copy(side).wait_send()

    for peer in range(cols):

        @pl.when(is_far[peer])
        def _(peer=peer):
            far_copy(peer).wait_send()
            fret_copy(peer).wait_send()

    k_factor = rates * rates * rates * x_finish(2) / full_width
    k_factor = to_columns(k_factor)[:, 1:2]
    dk_out[0, 0] = (k_rate * weighted - key_wide * k_factor).astype(BF16)


def body(sizes, q_raw, k_raw, values, upstream, outputs, logsumexp, gain_q, gain_k, far_list):
    rows, cols, parts = sizes
    tokens, width = q_raw.shape[2:]
    heads = logsumexp.shape[2]
    kb = tokens // UNITS
    delta_rows = -(-heads // 8) * 8
    shape = jax.ShapeDtypeStruct(q_raw.shape, BF16)
    vmem = pl.BlockSpec(memory_space=pltpu.VMEM)
    anywhere = pl.BlockSpec(memory_space=pl.ANY)
    tile = pltpu.VMEM((tokens, width), BF16)
    pair = (2, tokens, width)
    dma = pltpu.SemaphoreType.DMA
    return pl.pallas_call(
        functools.partial(kernel, sizes),
        out_shape=(shape, shape, shape),
        in_specs=[anywhere] * 5 + [vmem] * 3 + [pl.BlockSpec(memory_space=pltpu.SMEM)],
        out_specs=(vmem, vmem, vmem),
        scratch_shapes=[
            tile,
            tile,
            tile,
            tile,
            tile,
            tile,
            tile,
            pltpu.VMEM((delta_rows, tokens), F32),
            pltpu.VMEM((tokens, width), F32),
            pltpu.VMEM((8, 128), F32),
            pltpu.VMEM((4,) + pair, BF16),
            pltpu.VMEM((cols, 2, kb, width), BF16),
            pltpu.VMEM((cols, 2, kb, width), BF16),
            pltpu.VMEM((4,) + pair, BF16),
            pltpu.VMEM((4,) + pair, BF16),
            pltpu.VMEM((cols, 2, kb, width), BF16),
            pltpu.VMEM((cols, 2, kb, width), BF16),
            pltpu.VMEM(pair, F32),
            pltpu.VMEM((3, parts, 8, 128), F32),
            dma((5,)),
            dma((4, 2)),
            dma((4, 2)),
            dma((cols,)),
            dma((cols,)),
            dma((4,)),
            dma((4,)),
            dma((cols,)),
            dma((cols,)),
            dma((3, parts)),
            dma((3, parts)),
        ],
        compiler_params=pltpu.CompilerParams(collective_id=0, has_side_effects=True),
    )(
        q_raw,
        k_raw,
        values,
        upstream,
        outputs,
        logsumexp,
        gain_q.reshape(1, width),
        gain_k.reshape(1, width),
        far_list,
    )


def solution(mesh):
    sizes = (mesh.shape["ha"], mesh.shape["wa"], mesh.shape["hd"])
    tile = P("ha", "wa", None, "hd")
    return jax.shard_map(
        functools.partial(body, sizes),
        mesh=mesh,
        in_specs=(tile,) * 5 + (P("ha", "wa", "hd", None), P("hd"), P("hd"), P("ha", None, None)),
        out_specs=(tile,) * 3,
        check_vma=False,
    )
```

```python
import functools
import math

import jax
import jax.numpy as jnp
from jax import lax
from jax.experimental import pallas as pl
from jax.experimental.pallas import tpu as pltpu
from jax.sharding import PartitionSpec as P

UNITS = 4
EPS = 1e-06
MESH = pl.DeviceIdType.MESH
LAST = (((1,), (1,)), ((), ()))
FIRST = (((0,), (0,)), ((), ()))
PLAIN = (((1,), (0,)), ((), ()))
UP, DOWN, LEFT, RIGHT = range(4)
F32 = jnp.float32
BF16 = jnp.bfloat16


def dot(a, b, dims):
    return lax.dot_general(a, b, dims, preferred_element_type=F32)


def kernel(
    sizes,
    q_hbm,
    k_hbm,
    v_hbm,
    u_hbm,
    o_hbm,
    lse_ref,
    gain_q_ref,
    gain_k_ref,
    far_ref,
    dq_out,
    dk_out,
    dv_out,
    q_raw,
    k_raw,
    vals,
    ups,
    outs,
    qn,
    kn,
    delta_ref,
    dq_acc,
    staged,
    out_sem,
    halo,
    far_pack,
    far_in,
    ret_out,
    ret_in,
    fret_out,
    fret_in,
    total,
    xbuf,
    load_sem,
    halo_send,
    halo_recv,
    far_send,
    far_recv,
    ret_send,
    ret_recv,
    fret_send,
    fret_recv,
    x_send,
    x_recv,
):
    rows, cols, parts = sizes
    row = lax.axis_index("ha")
    col = lax.axis_index("wa")
    me = lax.axis_index("hd")
    tokens, width = q_raw.shape
    heads = lse_ref.shape[1]
    hw = width // heads
    kb = tokens // UNITS
    full_width = width * parts
    slots = far_ref.shape[2]
    score_scale = 1.0 / math.sqrt(hw)

    loads = []
    for index, (source, target) in enumerate(
        ((v_hbm, vals), (k_hbm, k_raw), (q_hbm, q_raw), (u_hbm, ups), (o_hbm, outs))
    ):
        copy = pltpu.make_async_copy(source.at[0, 0], target, load_sem.at[index])
        copy.start()
        loads.append(copy)

    out_copies = [
        pltpu.make_async_copy(staged.at[index], target.at[0, 0], out_sem.at[index])
        for index, target in enumerate((dq_out, dk_out, dv_out))
    ]
    exists = (row > 0, row < rows - 1, col > 0, col < cols - 1)
    ids = ({"ha": row - 1}, {"ha": row + 1}, {"wa": col - 1}, {"wa": col + 1})
    is_far = [(col - peer) * (col - peer) >= 4 for peer in range(cols)]

    barrier = pltpu.get_barrier_semaphore()
    hd_ids = [{"hd": lax.rem(me + off, parts)} for off in range(1, parts)]
    for target in hd_ids:
        pl.semaphore_signal(barrier, inc=1, device_id=target, device_id_type=MESH)
    for side in range(4):

        @pl.when(exists[side])
        def _(side=side):
            pl.semaphore_signal(barrier, inc=1, device_id=ids[side], device_id_type=MESH)

    for peer in range(cols):

        @pl.when(is_far[peer])
        def _(peer=peer):
            pl.semaphore_signal(barrier, inc=1, device_id={"wa": peer}, device_id_type=MESH)

    def lane_columns(columns):
        lane = lax.broadcasted_iota(jnp.int32, (tokens, 128), 1)
        mat = jnp.zeros((tokens, 128), F32)
        for place, column in columns:
            mat = jnp.where(lane == place, column, mat)
        return mat.T

    def row_sums(block):
        acc = block[:, :hw]
        for head in range(1, heads):
            acc = acc + block[:, head * hw : (head + 1) * hw]
        return jnp.sum(acc, axis=1, keepdims=True)

    def to_columns(rows8):
        return jnp.concatenate([rows8] * (tokens // 8), axis=0).T

    def x_copy(which, off):
        return pltpu.make_async_remote_copy(
            src_ref=xbuf.at[which, me],
            dst_ref=xbuf.at[which, me],
            send_sem=x_send.at[which, off],
            recv_sem=x_recv.at[which, off],
            device_id=hd_ids[off - 1],
            device_id_type=MESH,
        )

    def x_start(which, rows8):
        xbuf[which, me] = rows8
        for off in range(1, parts):
            x_copy(which, off).start()

    def x_finish(which):
        for off in range(1, parts):
            x_copy(which, off).wait()
        acc = xbuf[which, 0]
        for part in range(1, parts):
            acc = acc + xbuf[which, part]
        return acc

    def halo_copy(side, which, source):
        return pltpu.make_async_remote_copy(
            src_ref=source,
            dst_ref=halo.at[side ^ 1, which],
            send_sem=halo_send.at[side, which],
            recv_sem=halo_recv.at[side ^ 1, which],
            device_id=ids[side],
            device_id_type=MESH,
        )

    def halo_wait(side, which):
        pltpu.make_async_remote_copy(
            src_ref=vals,
            dst_ref=halo.at[side, which],
            send_sem=halo_send.at[side, which],
            recv_sem=halo_recv.at[side, which],
            device_id=ids[side],
            device_id_type=MESH,
        ).wait_recv()

    def far_copy(peer):
        return pltpu.make_async_remote_copy(
            src_ref=far_pack.at[peer],
            dst_ref=far_in.at[col],
            send_sem=far_send.at[peer],
            recv_sem=far_recv.at[col],
            device_id={"wa": peer},
            device_id_type=MESH,
        )

    def far_wait(peer):
        pltpu.make_async_remote_copy(
            src_ref=far_pack.at[peer],
            dst_ref=far_in.at[peer],
            send_sem=far_send.at[peer],
            recv_sem=far_recv.at[peer],
            device_id={"wa": peer},
            device_id_type=MESH,
        ).wait_recv()

    def ret_copy(side):
        return pltpu.make_async_remote_copy(
            src_ref=ret_out.at[side],
            dst_ref=ret_in.at[side ^ 1],
            send_sem=ret_send.at[side],
            recv_sem=ret_recv.at[side ^ 1],
            device_id=ids[side],
            device_id_type=MESH,
        )

    def ret_wait(side):
        pltpu.make_async_remote_copy(
            src_ref=ret_out.at[side],
            dst_ref=ret_in.at[side],
            send_sem=ret_send.at[side],
            recv_sem=ret_recv.at[side],
            device_id=ids[side],
            device_id_type=MESH,
        ).wait_recv()

    def fret_copy(peer):
        return pltpu.make_async_remote_copy(
            src_ref=fret_out.at[peer],
            dst_ref=fret_in.at[col],
            send_sem=fret_send.at[peer],
            recv_sem=fret_recv.at[col],
            device_id={"wa": peer},
            device_id_type=MESH,
        )

    def fret_wait(peer):
        pltpu.make_async_remote_copy(
            src_ref=fret_out.at[peer],
            dst_ref=fret_in.at[peer],
            send_sem=fret_send.at[peer],
            recv_sem=fret_recv.at[peer],
            device_id={"wa": peer},
            device_id_type=MESH,
        ).wait_recv()

    loads[0].wait()
    pl.semaphore_wait(
        barrier,
        parts
        - 1
        + jnp.minimum(row, 1)
        + jnp.minimum(rows - 1 - row, 1)
        + (cols - 1),
    )
    for side in range(4):

        @pl.when(exists[side])
        def _(side=side):
            halo_copy(side, 1, vals).start()

    loads[1].wait()
    key_wide = k_raw[...].astype(F32)
    key_squares = row_sums(key_wide * key_wide)
    loads[2].wait()
    query_wide = q_raw[...].astype(F32)
    query_squares = row_sums(query_wide * query_wide)
    sums = lane_columns([(0, query_squares), (1, key_squares)])[0:8]
    x_start(0, sums)

    loads[3].wait()
    loads[4].wait()
    delta_columns = []
    for head in range(heads):
        lanes = slice(head * hw, (head + 1) * hw)
        product = ups[:, lanes].astype(F32) * outs[:, lanes].astype(F32)
        delta_columns.append((head, jnp.sum(product, axis=1, keepdims=True)))
    delta_ref[...] = lane_columns(delta_columns)[0 : delta_ref.shape[0]]

    mine_used = []
    send_unit = []
    send_used = []
    for peer in range(cols):
        used = jnp.int32(0)
        unit = jnp.int32(0)
        asked = jnp.int32(0)
        for slot in range(slots):
            named = far_ref[0, col, slot] - peer * UNITS
            used = jnp.where((named >= 0) & (named < UNITS), 1, used)
            wanted = far_ref[0, peer, slot] - col * UNITS
            hit = (wanted >= 0) & (wanted < UNITS)
            unit = jnp.where(hit, wanted, unit)
            asked = jnp.where(hit, 1, asked)
        mine_used.append(used)
        send_unit.append(unit)
        send_used.append(asked)

    def pick_unit(peer, source):
        wanted = jnp.full((kb, width), send_unit[peer], jnp.int32)
        picked = source[0:kb, :].astype(F32)
        for unit in range(1, UNITS):
            block = source[unit * kb : (unit + 1) * kb, :].astype(F32)
            picked = jnp.where(wanted == unit, block, picked)
        return picked.astype(BF16)

    for peer in range(cols):

        @pl.when(is_far[peer])
        def _(peer=peer):
            far_pack[peer, 1] = pick_unit(peer, vals)

        @pl.when(jnp.logical_not(is_far[peer]))
        def _(peer=peer):
            far_in[peer] = jnp.zeros(far_in.shape[1:], BF16)

    gain_q = gain_q_ref[...].astype(F32).reshape(1, width)
    gain_k = gain_k_ref[...].astype(F32).reshape(1, width)
    rates = lax.rsqrt(x_finish(0) / full_width + EPS)
    rate_columns = to_columns(rates)
    q_rate = rate_columns[:, 0:1]
    k_rate = rate_columns[:, 1:2]
    kn[...] = (k_raw[...].astype(F32) * k_rate * gain_k).astype(BF16)
    for side in range(4):

        @pl.when(exists[side])
        def _(side=side):
            halo_copy(side, 0, kn).start()

    for peer in range(cols):

        @pl.when(is_far[peer])
        def _(peer=peer):
            far_pack[peer, 0] = pick_unit(peer, kn)
            far_copy(peer).start()

    qn[...] = (q_raw[...].astype(F32) * q_rate * gain_q).astype(BF16)

    def attend(head, key_head, value_head, mask):
        lanes = slice(head * hw, (head + 1) * hw)
        query_head = qn[:, lanes]
        upstream_head = ups[:, lanes]
        scores = dot(key_head, query_head, LAST) * score_scale
        weight = jnp.exp(scores - lse_ref[0, head])
        if mask is not None:
            weight = jnp.where(mask, weight, 0.0)
        dweight = dot(value_head, upstream_head, LAST)
        dscore = (weight * (dweight - delta_ref[head : head + 1, :])).astype(BF16)
        dq_part = dot(dscore, key_head, FIRST)
        dk_part = (dot(dscore, query_head, PLAIN) * score_scale).astype(BF16)
        dv_part = dot(weight.astype(BF16), upstream_head, PLAIN).astype(BF16)
        return dq_part, dk_part, dv_part

    for head in range(heads):
        lanes = slice(head * hw, (head + 1) * hw)
        dq_part, dk_part, dv_part = attend(head, kn[:, lanes], vals[:, lanes], None)
        dq_acc[:, lanes] = dq_part
        total[0, :, lanes] = dk_part.astype(F32)
        total[1, :, lanes] = dv_part.astype(F32)

    for side in range(4):

        @pl.when(exists[side])
        def _(side=side):
            halo_wait(side, 1)
            halo_wait(side, 0)
            for head in range(heads):
                lanes = slice(head * hw, (head + 1) * hw)
                dq_part, dk_part, dv_part = attend(
                    head, halo[side, 0, :, lanes], halo[side, 1, :, lanes], None
                )
                dq_acc[:, lanes] += dq_part
                ret_out[side, 0, :, lanes] = dk_part
                ret_out[side, 1, :, lanes] = dv_part
            ret_copy(side).start()

    for peer in range(cols):

        @pl.when(is_far[peer])
        def _(peer=peer):
            far_wait(peer)

    mask = jnp.concatenate(
        [jnp.full((kb, tokens), used, jnp.int32) for used in mine_used], axis=0
    ) > 0
    for head in range(heads):
        lanes = slice(head * hw, (head + 1) * hw)
        dq_part, dk_part, dv_part = attend(
            head,
            far_in[:, 0, :, lanes].reshape(cols * kb, hw),
            far_in[:, 1, :, lanes].reshape(cols * kb, hw),
            mask,
        )
        dq_acc[:, lanes] += dq_part
        fret_out[:, 0, :, lanes] = dk_part.reshape(cols, kb, hw)
        fret_out[:, 1, :, lanes] = dv_part.reshape(cols, kb, hw)
    for peer in range(cols):

        @pl.when(is_far[peer])
        def _(peer=peer):
            fret_copy(peer).start()

    dq_norm = (dq_acc[...] * score_scale).astype(BF16).astype(F32)
    query_wide = q_raw[...].astype(F32)
    weighted = gain_q * dq_norm
    x_start(1, lane_columns([(0, row_sums(weighted * query_wide))])[0:8])
    q_factor = rates * rates * rates * x_finish(1) / full_width
    q_factor = to_columns(q_factor)[:, 0:1]
    staged[0] = (q_rate * weighted - query_wide * q_factor).astype(BF16)
    out_copies[0].start()

    for side in range(4):

        @pl.when(exists[side])
        def _(side=side):
            ret_wait(side)
            total[...] += ret_in[side].astype(F32)

    for peer in range(cols):

        @pl.when(is_far[peer])
        def _(peer=peer):
            fret_wait(peer)
            for unit in range(UNITS):
                picked = jnp.where(send_unit[peer] == unit, send_used[peer], 0)
                spread = jnp.full((kb, width), picked, jnp.int32) > 0
                place = slice(unit * kb, (unit + 1) * kb)
                for which in range(2):
                    total[which, place, :] += jnp.where(
                        spread, fret_in[peer, which].astype(F32), 0.0
                    )

    dk_norm = total[0].astype(BF16).astype(F32)
    key_wide = k_raw[...].astype(F32)
    weighted = gain_k * dk_norm
    x_start(2, lane_columns([(1, row_sums(weighted * key_wide))])[0:8])
    staged[2] = total[1].astype(BF16)
    out_copies[2].start()
    for side in range(4):

        @pl.when(exists[side])
        def _(side=side):
            halo_copy(side, 1, vals).wait_send()
            halo_copy(side, 0, kn).wait_send()
            ret_copy(side).wait_send()

    for peer in range(cols):

        @pl.when(is_far[peer])
        def _(peer=peer):
            far_copy(peer).wait_send()
            fret_copy(peer).wait_send()

    k_factor = rates * rates * rates * x_finish(2) / full_width
    k_factor = to_columns(k_factor)[:, 1:2]
    staged[1] = (k_rate * weighted - key_wide * k_factor).astype(BF16)
    out_copies[1].start()
    for copy in out_copies:
        copy.wait()


def copy_kernel(dq_in, dk_in, dv_in, dq_out, dk_out, dv_out, stage, in_sem, out_sem):
    pairs = ((dq_in, dq_out), (dv_in, dv_out), (dk_in, dk_out))
    into = []
    back = []
    for index, (source, target) in enumerate(pairs):
        into.append(pltpu.make_async_copy(source, stage.at[index], in_sem.at[index]))
        back.append(pltpu.make_async_copy(stage.at[index], target, out_sem.at[index]))
    for copy in into:
        copy.start()
    for first, second in zip(into, back):
        first.wait()
        second.start()
    for copy in back:
        copy.wait()


def body(sizes, q_raw, k_raw, values, upstream, outputs, logsumexp, gain_q, gain_k, far_list):
    rows, cols, parts = sizes
    tokens, width = q_raw.shape[2:]
    heads = logsumexp.shape[2]
    kb = tokens // UNITS
    delta_rows = -(-heads // 8) * 8
    shape = jax.ShapeDtypeStruct(q_raw.shape, BF16)
    vmem = pl.BlockSpec(memory_space=pltpu.VMEM)
    anywhere = pl.BlockSpec(memory_space=pltpu.HBM)
    tile = pltpu.VMEM((tokens, width), BF16)
    pair = (2, tokens, width)
    dma = pltpu.SemaphoreType.DMA
    grads = pl.pallas_call(
        functools.partial(kernel, sizes),
        out_shape=(shape, shape, shape),
        in_specs=[anywhere] * 5 + [vmem] * 3 + [pl.BlockSpec(memory_space=pltpu.SMEM)],
        out_specs=(anywhere,) * 3,
        scratch_shapes=[
            tile,
            tile,
            tile,
            tile,
            tile,
            tile,
            tile,
            pltpu.VMEM((delta_rows, tokens), F32),
            pltpu.VMEM((tokens, width), F32),
            pltpu.VMEM((3, tokens, width), BF16),
            dma((3,)),
            pltpu.VMEM((4,) + pair, BF16),
            pltpu.VMEM((cols, 2, kb, width), BF16),
            pltpu.VMEM((cols, 2, kb, width), BF16),
            pltpu.VMEM((4,) + pair, BF16),
            pltpu.VMEM((4,) + pair, BF16),
            pltpu.VMEM((cols, 2, kb, width), BF16),
            pltpu.VMEM((cols, 2, kb, width), BF16),
            pltpu.VMEM(pair, F32),
            pltpu.VMEM((3, parts, 8, 128), F32),
            dma((5,)),
            dma((4, 2)),
            dma((4, 2)),
            dma((cols,)),
            dma((cols,)),
            dma((4,)),
            dma((4,)),
            dma((cols,)),
            dma((cols,)),
            dma((3, parts)),
            dma((3, parts)),
        ],
        compiler_params=pltpu.CompilerParams(collective_id=0, has_side_effects=True),
    )(
        q_raw,
        k_raw,
        values,
        upstream,
        outputs,
        logsumexp.transpose(0, 2, 1, 3),
        gain_q,
        gain_k,
        far_list,
    )
    return pl.pallas_call(
        copy_kernel,
        out_shape=(shape, shape, shape),
        in_specs=[anywhere] * 3,
        out_specs=(anywhere,) * 3,
        scratch_shapes=[pltpu.VMEM((3,) + q_raw.shape, BF16), dma((3,)), dma((3,))],
    )(*grads)


def solution(mesh):
    sizes = (mesh.shape["ha"], mesh.shape["wa"], mesh.shape["hd"])
    tile = P("ha", "wa", None, "hd")
    return jax.shard_map(
        functools.partial(body, sizes),
        mesh=mesh,
        in_specs=(tile,) * 5 + (P("ha", "wa", "hd", None), P("hd"), P("hd"), P("ha", None, None)),
        out_specs=(tile,) * 3,
        check_vma=False,
    )
```

```python
import functools
import math

import jax
import jax.numpy as jnp
from jax import lax
from jax.experimental import pallas as pl
from jax.experimental.pallas import tpu as pltpu
from jax.sharding import PartitionSpec as P

UNITS = 4
EPS = 1e-06
MESH = pl.DeviceIdType.MESH
LAST = (((1,), (1,)), ((), ()))
FIRST = (((0,), (0,)), ((), ()))
PLAIN = (((1,), (0,)), ((), ()))
UP, DOWN, LEFT, RIGHT = range(4)
F32 = jnp.float32
BF16 = jnp.bfloat16


def dot(a, b, dims):
    return lax.dot_general(a, b, dims, preferred_element_type=F32)


def kernel(
    sizes,
    q_hbm,
    k_hbm,
    v_hbm,
    u_hbm,
    o_hbm,
    lse_ref,
    gain_q_ref,
    gain_k_ref,
    far_ref,
    dq_out,
    dk_out,
    dv_out,
    q_raw,
    k_raw,
    vals,
    ups,
    outs,
    qn,
    kn,
    delta_ref,
    dq_acc,
    halo,
    far_pack,
    far_in,
    ret_out,
    ret_in,
    fret_out,
    fret_in,
    total,
    xbuf,
    load_sem,
    halo_send,
    halo_recv,
    far_send,
    far_recv,
    ret_send,
    ret_recv,
    fret_send,
    fret_recv,
    x_send,
    x_recv,
):
    rows, cols, parts = sizes
    row = lax.axis_index("ha")
    col = lax.axis_index("wa")
    me = lax.axis_index("hd")
    tokens, width = q_raw.shape
    heads = lse_ref.shape[1]
    hw = width // heads
    kb = tokens // UNITS
    full_width = width * parts
    slots = far_ref.shape[2]
    score_scale = 1.0 / math.sqrt(hw)

    loads = []
    for index, (source, target) in enumerate(
        ((v_hbm, vals), (k_hbm, k_raw), (q_hbm, q_raw), (u_hbm, ups), (o_hbm, outs))
    ):
        copy = pltpu.make_async_copy(source.at[0, 0], target, load_sem.at[index])
        copy.start()
        loads.append(copy)

    exists = (row > 0, row < rows - 1, col > 0, col < cols - 1)
    ids = ({"ha": row - 1}, {"ha": row + 1}, {"wa": col - 1}, {"wa": col + 1})
    is_far = [(col - peer) * (col - peer) >= 4 for peer in range(cols)]

    barrier = pltpu.get_barrier_semaphore()
    hd_ids = [{"hd": lax.rem(me + off, parts)} for off in range(1, parts)]
    for target in hd_ids:
        pl.semaphore_signal(barrier, inc=1, device_id=target, device_id_type=MESH)
    for side in range(4):

        @pl.when(exists[side])
        def _(side=side):
            pl.semaphore_signal(barrier, inc=1, device_id=ids[side], device_id_type=MESH)

    for peer in range(cols):

        @pl.when(is_far[peer])
        def _(peer=peer):
            pl.semaphore_signal(barrier, inc=1, device_id={"wa": peer}, device_id_type=MESH)

    def lane_columns(columns):
        lane = lax.broadcasted_iota(jnp.int32, (tokens, 128), 1)
        mat = jnp.zeros((tokens, 128), F32)
        for place, column in columns:
            mat = jnp.where(lane == place, column, mat)
        return mat.T

    def row_sums(block):
        acc = block[:, :hw]
        for head in range(1, heads):
            acc = acc + block[:, head * hw : (head + 1) * hw]
        return jnp.sum(acc, axis=1, keepdims=True)

    def to_columns(rows8):
        return jnp.concatenate([rows8] * (tokens // 8), axis=0).T

    def x_copy(which, off):
        return pltpu.make_async_remote_copy(
            src_ref=xbuf.at[which, me],
            dst_ref=xbuf.at[which, me],
            send_sem=x_send.at[which, off],
            recv_sem=x_recv.at[which, off],
            device_id=hd_ids[off - 1],
            device_id_type=MESH,
        )

    def x_start(which, rows8):
        xbuf[which, me] = rows8
        for off in range(1, parts):
            x_copy(which, off).start()

    def x_finish(which):
        for off in range(1, parts):
            x_copy(which, off).wait()
        acc = xbuf[which, 0]
        for part in range(1, parts):
            acc = acc + xbuf[which, part]
        return acc

    def halo_copy(side, which, source):
        return pltpu.make_async_remote_copy(
            src_ref=source,
            dst_ref=halo.at[side ^ 1, which],
            send_sem=halo_send.at[side, which],
            recv_sem=halo_recv.at[side ^ 1, which],
            device_id=ids[side],
            device_id_type=MESH,
        )

    def halo_wait(side, which):
        pltpu.make_async_remote_copy(
            src_ref=vals,
            dst_ref=halo.at[side, which],
            send_sem=halo_send.at[side, which],
            recv_sem=halo_recv.at[side, which],
            device_id=ids[side],
            device_id_type=MESH,
        ).wait_recv()

    def far_copy(peer):
        return pltpu.make_async_remote_copy(
            src_ref=far_pack.at[peer],
            dst_ref=far_in.at[col],
            send_sem=far_send.at[peer],
            recv_sem=far_recv.at[col],
            device_id={"wa": peer},
            device_id_type=MESH,
        )

    def far_wait(peer):
        pltpu.make_async_remote_copy(
            src_ref=far_pack.at[peer],
            dst_ref=far_in.at[peer],
            send_sem=far_send.at[peer],
            recv_sem=far_recv.at[peer],
            device_id={"wa": peer},
            device_id_type=MESH,
        ).wait_recv()

    def ret_copy(side):
        return pltpu.make_async_remote_copy(
            src_ref=ret_out.at[side],
            dst_ref=ret_in.at[side ^ 1],
            send_sem=ret_send.at[side],
            recv_sem=ret_recv.at[side ^ 1],
            device_id=ids[side],
            device_id_type=MESH,
        )

    def ret_wait(side):
        pltpu.make_async_remote_copy(
            src_ref=ret_out.at[side],
            dst_ref=ret_in.at[side],
            send_sem=ret_send.at[side],
            recv_sem=ret_recv.at[side],
            device_id=ids[side],
            device_id_type=MESH,
        ).wait_recv()

    def fret_copy(peer):
        return pltpu.make_async_remote_copy(
            src_ref=fret_out.at[peer],
            dst_ref=fret_in.at[col],
            send_sem=fret_send.at[peer],
            recv_sem=fret_recv.at[col],
            device_id={"wa": peer},
            device_id_type=MESH,
        )

    def fret_wait(peer):
        pltpu.make_async_remote_copy(
            src_ref=fret_out.at[peer],
            dst_ref=fret_in.at[peer],
            send_sem=fret_send.at[peer],
            recv_sem=fret_recv.at[peer],
            device_id={"wa": peer},
            device_id_type=MESH,
        ).wait_recv()

    loads[0].wait()
    pl.semaphore_wait(
        barrier,
        parts
        - 1
        + jnp.minimum(row, 1)
        + jnp.minimum(rows - 1 - row, 1)
        + (cols - 1),
    )
    for side in range(4):

        @pl.when(exists[side])
        def _(side=side):
            halo_copy(side, 1, vals).start()

    loads[1].wait()
    key_wide = k_raw[...].astype(F32)
    key_squares = row_sums(key_wide * key_wide)
    loads[2].wait()
    query_wide = q_raw[...].astype(F32)
    query_squares = row_sums(query_wide * query_wide)
    sums = lane_columns([(0, query_squares), (1, key_squares)])[0:8]
    x_start(0, sums)

    loads[3].wait()
    loads[4].wait()
    delta_columns = []
    for head in range(heads):
        lanes = slice(head * hw, (head + 1) * hw)
        product = ups[:, lanes].astype(F32) * outs[:, lanes].astype(F32)
        delta_columns.append((head, jnp.sum(product, axis=1, keepdims=True)))
    delta_ref[...] = lane_columns(delta_columns)[0 : delta_ref.shape[0]]

    mine_used = []
    send_unit = []
    send_used = []
    for peer in range(cols):
        used = jnp.int32(0)
        unit = jnp.int32(0)
        asked = jnp.int32(0)
        for slot in range(slots):
            named = far_ref[0, col, slot] - peer * UNITS
            used = jnp.where((named >= 0) & (named < UNITS), 1, used)
            wanted = far_ref[0, peer, slot] - col * UNITS
            hit = (wanted >= 0) & (wanted < UNITS)
            unit = jnp.where(hit, wanted, unit)
            asked = jnp.where(hit, 1, asked)
        mine_used.append(used)
        send_unit.append(unit)
        send_used.append(asked)

    def pick_unit(peer, source):
        wanted = jnp.full((kb, width), send_unit[peer], jnp.int32)
        picked = source[0:kb, :].astype(F32)
        for unit in range(1, UNITS):
            block = source[unit * kb : (unit + 1) * kb, :].astype(F32)
            picked = jnp.where(wanted == unit, block, picked)
        return picked.astype(BF16)

    for peer in range(cols):

        @pl.when(is_far[peer])
        def _(peer=peer):
            far_pack[peer, 1] = pick_unit(peer, vals)

        @pl.when(jnp.logical_not(is_far[peer]))
        def _(peer=peer):
            far_in[peer] = jnp.zeros(far_in.shape[1:], BF16)

    gain_q = gain_q_ref[...].astype(F32).reshape(1, width)
    gain_k = gain_k_ref[...].astype(F32).reshape(1, width)
    rates = lax.rsqrt(x_finish(0) / full_width + EPS)
    rate_columns = to_columns(rates)
    q_rate = rate_columns[:, 0:1]
    k_rate = rate_columns[:, 1:2]
    kn[...] = (k_raw[...].astype(F32) * k_rate * gain_k).astype(BF16)
    for side in range(4):

        @pl.when(exists[side])
        def _(side=side):
            halo_copy(side, 0, kn).start()

    for peer in range(cols):

        @pl.when(is_far[peer])
        def _(peer=peer):
            far_pack[peer, 0] = pick_unit(peer, kn)
            far_copy(peer).start()

    qn[...] = (q_raw[...].astype(F32) * q_rate * gain_q).astype(BF16)

    def attend(head, key_head, value_head, mask):
        lanes = slice(head * hw, (head + 1) * hw)
        query_head = qn[:, lanes]
        upstream_head = ups[:, lanes]
        scores = dot(key_head, query_head, LAST) * score_scale
        weight = jnp.exp(scores - lse_ref[0, head])
        if mask is not None:
            weight = jnp.where(mask, weight, 0.0)
        dweight = dot(value_head, upstream_head, LAST)
        dscore = (weight * (dweight - delta_ref[head : head + 1, :])).astype(BF16)
        dq_part = dot(dscore, key_head, FIRST)
        dk_part = (dot(dscore, query_head, PLAIN) * score_scale).astype(BF16)
        dv_part = dot(weight.astype(BF16), upstream_head, PLAIN).astype(BF16)
        return dq_part, dk_part, dv_part

    for head in range(heads):
        lanes = slice(head * hw, (head + 1) * hw)
        dq_part, dk_part, dv_part = attend(head, kn[:, lanes], vals[:, lanes], None)
        dq_acc[:, lanes] = dq_part
        total[0, :, lanes] = dk_part.astype(F32)
        total[1, :, lanes] = dv_part.astype(F32)

    for side in range(4):

        @pl.when(exists[side])
        def _(side=side):
            halo_wait(side, 1)
            halo_wait(side, 0)
            for head in range(heads):
                lanes = slice(head * hw, (head + 1) * hw)
                dq_part, dk_part, dv_part = attend(
                    head, halo[side, 0, :, lanes], halo[side, 1, :, lanes], None
                )
                dq_acc[:, lanes] += dq_part
                ret_out[side, 0, :, lanes] = dk_part
                ret_out[side, 1, :, lanes] = dv_part
            ret_copy(side).start()

    for peer in range(cols):

        @pl.when(is_far[peer])
        def _(peer=peer):
            far_wait(peer)

    mask = jnp.concatenate(
        [jnp.full((kb, tokens), used, jnp.int32) for used in mine_used], axis=0
    ) > 0
    for head in range(heads):
        lanes = slice(head * hw, (head + 1) * hw)
        dq_part, dk_part, dv_part = attend(
            head,
            far_in[:, 0, :, lanes].reshape(cols * kb, hw),
            far_in[:, 1, :, lanes].reshape(cols * kb, hw),
            mask,
        )
        dq_acc[:, lanes] += dq_part
        fret_out[:, 0, :, lanes] = dk_part.reshape(cols, kb, hw)
        fret_out[:, 1, :, lanes] = dv_part.reshape(cols, kb, hw)
    for peer in range(cols):

        @pl.when(is_far[peer])
        def _(peer=peer):
            fret_copy(peer).start()

    dq_norm = (dq_acc[...] * score_scale).astype(BF16).astype(F32)
    query_wide = q_raw[...].astype(F32)
    weighted = gain_q * dq_norm
    x_start(1, lane_columns([(0, row_sums(weighted * query_wide))])[0:8])
    q_factor = rates * rates * rates * x_finish(1) / full_width
    q_factor = to_columns(q_factor)[:, 0:1]
    dq_out[0, 0] = (q_rate * weighted - query_wide * q_factor).astype(BF16)

    for side in range(4):

        @pl.when(exists[side])
        def _(side=side):
            ret_wait(side)
            total[...] += ret_in[side].astype(F32)

    for peer in range(cols):

        @pl.when(is_far[peer])
        def _(peer=peer):
            fret_wait(peer)
            for unit in range(UNITS):
                picked = jnp.where(send_unit[peer] == unit, send_used[peer], 0)
                spread = jnp.full((kb, width), picked, jnp.int32) > 0
                place = slice(unit * kb, (unit + 1) * kb)
                for which in range(2):
                    total[which, place, :] += jnp.where(
                        spread, fret_in[peer, which].astype(F32), 0.0
                    )

    dk_norm = total[0].astype(BF16).astype(F32)
    key_wide = k_raw[...].astype(F32)
    weighted = gain_k * dk_norm
    x_start(2, lane_columns([(1, row_sums(weighted * key_wide))])[0:8])
    dv_out[0, 0] = total[1].astype(BF16)
    for side in range(4):

        @pl.when(exists[side])
        def _(side=side):
            halo_copy(side, 1, vals).wait_send()
            halo_copy(side, 0, kn).wait_send()
            ret_copy(side).wait_send()

    for peer in range(cols):

        @pl.when(is_far[peer])
        def _(peer=peer):
            far_copy(peer).wait_send()
            fret_copy(peer).wait_send()

    k_factor = rates * rates * rates * x_finish(2) / full_width
    k_factor = to_columns(k_factor)[:, 1:2]
    dk_out[0, 0] = (k_rate * weighted - key_wide * k_factor).astype(BF16)


def copy_kernel(dq_in, dk_in, dv_in, dq_out, dk_out, dv_out, sem):
    pairs = ((dq_in, dq_out), (dk_in, dk_out), (dv_in, dv_out))
    copies = [
        pltpu.make_async_copy(source, target, sem.at[index])
        for index, (source, target) in enumerate(pairs)
    ]
    for copy in copies:
        copy.start()
    for copy in copies:
        copy.wait()


def body(sizes, q_raw, k_raw, values, upstream, outputs, logsumexp, gain_q, gain_k, far_list):
    rows, cols, parts = sizes
    tokens, width = q_raw.shape[2:]
    heads = logsumexp.shape[2]
    kb = tokens // UNITS
    delta_rows = -(-heads // 8) * 8
    shape = jax.ShapeDtypeStruct(q_raw.shape, BF16)
    vmem = pl.BlockSpec(memory_space=pltpu.VMEM)
    anywhere = pl.BlockSpec(memory_space=pltpu.HBM)
    tile = pltpu.VMEM((tokens, width), BF16)
    pair = (2, tokens, width)
    dma = pltpu.SemaphoreType.DMA
    grads = pl.pallas_call(
        functools.partial(kernel, sizes),
        out_shape=(pltpu.VMEM(q_raw.shape, BF16),) * 3,
        in_specs=[anywhere] * 5 + [vmem] * 3 + [pl.BlockSpec(memory_space=pltpu.SMEM)],
        out_specs=(vmem,) * 3,
        scratch_shapes=[
            tile,
            tile,
            tile,
            tile,
            tile,
            tile,
            tile,
            pltpu.VMEM((delta_rows, tokens), F32),
            pltpu.VMEM((tokens, width), F32),
            pltpu.VMEM((4,) + pair, BF16),
            pltpu.VMEM((cols, 2, kb, width), BF16),
            pltpu.VMEM((cols, 2, kb, width), BF16),
            pltpu.VMEM((4,) + pair, BF16),
            pltpu.VMEM((4,) + pair, BF16),
            pltpu.VMEM((cols, 2, kb, width), BF16),
            pltpu.VMEM((cols, 2, kb, width), BF16),
            pltpu.VMEM(pair, F32),
            pltpu.VMEM((3, parts, 8, 128), F32),
            dma((5,)),
            dma((4, 2)),
            dma((4, 2)),
            dma((cols,)),
            dma((cols,)),
            dma((4,)),
            dma((4,)),
            dma((cols,)),
            dma((cols,)),
            dma((3, parts)),
            dma((3, parts)),
        ],
        compiler_params=pltpu.CompilerParams(collective_id=0, has_side_effects=True),
    )(
        q_raw,
        k_raw,
        values,
        upstream,
        outputs,
        logsumexp.transpose(0, 2, 1, 3),
        gain_q,
        gain_k,
        far_list,
    )
    return pl.pallas_call(
        copy_kernel,
        out_shape=(shape, shape, shape),
        in_specs=[vmem] * 3,
        out_specs=(anywhere,) * 3,
        scratch_shapes=[dma((3,))],
        compiler_params=pltpu.CompilerParams(vmem_limit_bytes=4 << 20),
    )(*grads)


def solution(mesh):
    sizes = (mesh.shape["ha"], mesh.shape["wa"], mesh.shape["hd"])
    tile = P("ha", "wa", None, "hd")
    return jax.shard_map(
        functools.partial(body, sizes),
        mesh=mesh,
        in_specs=(tile,) * 5 + (P("ha", "wa", "hd", None), P("hd"), P("hd"), P("ha", None, None)),
        out_specs=(tile,) * 3,
        check_vma=False,
    )
```

```python
import functools
import math

import jax
import jax.numpy as jnp
from jax import lax
from jax.experimental import pallas as pl
from jax.experimental.pallas import tpu as pltpu
from jax.sharding import PartitionSpec as P

UNITS = 4
EPS = 1e-06
MESH = pl.DeviceIdType.MESH
LAST = (((1,), (1,)), ((), ()))
FIRST = (((0,), (0,)), ((), ()))
PLAIN = (((1,), (0,)), ((), ()))
UP, DOWN, LEFT, RIGHT = range(4)
F32 = jnp.float32
BF16 = jnp.bfloat16


def dot(a, b, dims):
    return lax.dot_general(a, b, dims, preferred_element_type=F32)


def kernel(
    sizes,
    q_hbm,
    k_hbm,
    v_hbm,
    u_hbm,
    o_hbm,
    lse_ref,
    gain_q_ref,
    gain_k_ref,
    far_ref,
    dq_out,
    dk_out,
    dv_out,
    q_raw,
    k_raw,
    vals,
    ups,
    outs,
    qn,
    kn,
    delta_ref,
    dq_acc,
    halo,
    far_pack,
    far_in,
    ret_out,
    ret_in,
    fret_out,
    fret_in,
    total,
    xbuf,
    load_sem,
    halo_send,
    halo_recv,
    far_send,
    far_recv,
    ret_send,
    ret_recv,
    fret_send,
    fret_recv,
    x_send,
    x_recv,
):
    rows, cols, parts = sizes
    row = lax.axis_index("ha")
    col = lax.axis_index("wa")
    me = lax.axis_index("hd")
    tokens, width = q_raw.shape
    heads = lse_ref.shape[1]
    hw = width // heads
    kb = tokens // UNITS
    full_width = width * parts
    slots = far_ref.shape[2]
    score_scale = 1.0 / math.sqrt(hw)

    loads = []
    for index, (source, target) in enumerate(
        ((v_hbm, vals), (k_hbm, k_raw), (q_hbm, q_raw), (u_hbm, ups), (o_hbm, outs))
    ):
        copy = pltpu.make_async_copy(source.at[0, 0], target, load_sem.at[index])
        copy.start()
        loads.append(copy)

    exists = (row > 0, row < rows - 1, col > 0, col < cols - 1)
    ids = ({"ha": row - 1}, {"ha": row + 1}, {"wa": col - 1}, {"wa": col + 1})
    is_far = [(col - peer) * (col - peer) >= 4 for peer in range(cols)]

    barrier = pltpu.get_barrier_semaphore()
    hd_ids = [{"hd": lax.rem(me + off, parts)} for off in range(1, parts)]
    for target in hd_ids:
        pl.semaphore_signal(barrier, inc=1, device_id=target, device_id_type=MESH)
    for side in range(4):

        @pl.when(exists[side])
        def _(side=side):
            pl.semaphore_signal(barrier, inc=1, device_id=ids[side], device_id_type=MESH)

    for peer in range(cols):

        @pl.when(is_far[peer])
        def _(peer=peer):
            pl.semaphore_signal(barrier, inc=1, device_id={"wa": peer}, device_id_type=MESH)

    def lane_columns(columns):
        lane = lax.broadcasted_iota(jnp.int32, (tokens, 128), 1)
        mat = jnp.zeros((tokens, 128), F32)
        for place, column in columns:
            mat = jnp.where(lane == place, column, mat)
        return mat.T

    def row_sums(block):
        acc = block[:, :hw]
        for head in range(1, heads):
            acc = acc + block[:, head * hw : (head + 1) * hw]
        return jnp.sum(acc, axis=1, keepdims=True)

    def to_columns(rows8):
        return jnp.concatenate([rows8] * (tokens // 8), axis=0).T

    def x_copy(which, off):
        return pltpu.make_async_remote_copy(
            src_ref=xbuf.at[which, me],
            dst_ref=xbuf.at[which, me],
            send_sem=x_send.at[which, off],
            recv_sem=x_recv.at[which, off],
            device_id=hd_ids[off - 1],
            device_id_type=MESH,
        )

    def x_start(which, rows8):
        xbuf[which, me] = rows8
        for off in range(1, parts):
            x_copy(which, off).start()

    def x_finish(which):
        for off in range(1, parts):
            x_copy(which, off).wait()
        acc = xbuf[which, 0]
        for part in range(1, parts):
            acc = acc + xbuf[which, part]
        return acc

    def halo_copy(side, which, source):
        return pltpu.make_async_remote_copy(
            src_ref=source,
            dst_ref=halo.at[side ^ 1, which],
            send_sem=halo_send.at[side, which],
            recv_sem=halo_recv.at[side ^ 1, which],
            device_id=ids[side],
            device_id_type=MESH,
        )

    def halo_wait(side, which):
        pltpu.make_async_remote_copy(
            src_ref=vals,
            dst_ref=halo.at[side, which],
            send_sem=halo_send.at[side, which],
            recv_sem=halo_recv.at[side, which],
            device_id=ids[side],
            device_id_type=MESH,
        ).wait_recv()

    def far_copy(peer, owner):
        return pltpu.make_async_remote_copy(
            src_ref=far_pack.at[peer],
            dst_ref=far_in.at[owner],
            send_sem=far_send.at[peer],
            recv_sem=far_recv.at[owner],
            device_id={"wa": peer},
            device_id_type=MESH,
        )

    def far_wait(peer):
        pltpu.make_async_remote_copy(
            src_ref=far_pack.at[peer],
            dst_ref=far_in.at[peer],
            send_sem=far_send.at[peer],
            recv_sem=far_recv.at[peer],
            device_id={"wa": peer},
            device_id_type=MESH,
        ).wait_recv()

    def ret_copy(side):
        return pltpu.make_async_remote_copy(
            src_ref=ret_out.at[side],
            dst_ref=ret_in.at[side ^ 1],
            send_sem=ret_send.at[side],
            recv_sem=ret_recv.at[side ^ 1],
            device_id=ids[side],
            device_id_type=MESH,
        )

    def ret_wait(side):
        pltpu.make_async_remote_copy(
            src_ref=ret_out.at[side],
            dst_ref=ret_in.at[side],
            send_sem=ret_send.at[side],
            recv_sem=ret_recv.at[side],
            device_id=ids[side],
            device_id_type=MESH,
        ).wait_recv()

    def fret_copy(peer):
        return pltpu.make_async_remote_copy(
            src_ref=fret_out.at[peer],
            dst_ref=fret_in.at[col],
            send_sem=fret_send.at[peer],
            recv_sem=fret_recv.at[col],
            device_id={"wa": peer},
            device_id_type=MESH,
        )

    def fret_wait(peer):
        pltpu.make_async_remote_copy(
            src_ref=fret_out.at[peer],
            dst_ref=fret_in.at[peer],
            send_sem=fret_send.at[peer],
            recv_sem=fret_recv.at[peer],
            device_id={"wa": peer},
            device_id_type=MESH,
        ).wait_recv()

    loads[0].wait()
    pl.semaphore_wait(
        barrier,
        parts
        - 1
        + jnp.minimum(row, 1)
        + jnp.minimum(rows - 1 - row, 1)
        + (cols - 1),
    )
    for side in range(4):

        @pl.when(exists[side])
        def _(side=side):
            halo_copy(side, 1, vals).start()

    loads[1].wait()
    key_wide = k_raw[...].astype(F32)
    key_squares = row_sums(key_wide * key_wide)
    loads[2].wait()
    query_wide = q_raw[...].astype(F32)
    query_squares = row_sums(query_wide * query_wide)
    sums = lane_columns([(0, query_squares), (1, key_squares)])[0:8]
    x_start(0, sums)

    loads[3].wait()
    loads[4].wait()
    delta_columns = []
    for head in range(heads):
        lanes = slice(head * hw, (head + 1) * hw)
        product = ups[:, lanes].astype(F32) * outs[:, lanes].astype(F32)
        delta_columns.append((head, jnp.sum(product, axis=1, keepdims=True)))
    delta_ref[...] = lane_columns(delta_columns)[0 : delta_ref.shape[0]]

    def unit_of(peer, owner):
        unit = jnp.int32(0)
        asked = jnp.int32(0)
        for slot in range(slots):
            wanted = far_ref[0, peer, slot] - owner * UNITS
            hit = (wanted >= 0) & (wanted < UNITS)
            unit = jnp.where(hit, wanted, unit)
            asked = jnp.where(hit, 1, asked)
        return unit, asked

    mine_used = [unit_of(col, peer)[1] for peer in range(cols)]
    send_unit, send_used = zip(*[unit_of(peer, col) for peer in range(cols)])
    beyond = {
        LEFT: [(peer > col) & (col > 0) for peer in range(cols)],
        RIGHT: [(peer < col) & (col < cols - 1) for peer in range(cols)],
    }
    owners = {LEFT: col - 1, RIGHT: col + 1}

    def pick_unit(unit_index, source):
        wanted = jnp.full((kb, width), unit_index, jnp.int32)
        picked = source[0:kb, :].astype(F32)
        for unit in range(1, UNITS):
            block = source[unit * kb : (unit + 1) * kb, :].astype(F32)
            picked = jnp.where(wanted == unit, block, picked)
        return picked.astype(BF16)

    for peer in range(cols):

        @pl.when(jnp.logical_not(is_far[peer]))
        def _(peer=peer):
            far_in[peer] = jnp.zeros(far_in.shape[1:], BF16)

    gain_q = gain_q_ref[...].astype(F32).reshape(1, width)
    gain_k = gain_k_ref[...].astype(F32).reshape(1, width)
    rates = lax.rsqrt(x_finish(0) / full_width + EPS)
    rate_columns = to_columns(rates)
    q_rate = rate_columns[:, 0:1]
    k_rate = rate_columns[:, 1:2]
    kn[...] = (k_raw[...].astype(F32) * k_rate * gain_k).astype(BF16)
    for side in range(4):

        @pl.when(exists[side])
        def _(side=side):
            halo_copy(side, 0, kn).start()

    qn[...] = (q_raw[...].astype(F32) * q_rate * gain_q).astype(BF16)

    def attend(head, key_head, value_head, mask):
        lanes = slice(head * hw, (head + 1) * hw)
        query_head = qn[:, lanes]
        upstream_head = ups[:, lanes]
        scores = dot(key_head, query_head, LAST) * score_scale
        weight = jnp.exp(scores - lse_ref[0, head])
        if mask is not None:
            weight = jnp.where(mask, weight, 0.0)
        dweight = dot(value_head, upstream_head, LAST)
        dscore = (weight * (dweight - delta_ref[head : head + 1, :])).astype(BF16)
        dq_part = dot(dscore, key_head, FIRST)
        dk_part = (dot(dscore, query_head, PLAIN) * score_scale).astype(BF16)
        dv_part = dot(weight.astype(BF16), upstream_head, PLAIN).astype(BF16)
        return dq_part, dk_part, dv_part

    for head in range(heads):
        lanes = slice(head * hw, (head + 1) * hw)
        dq_part, dk_part, dv_part = attend(head, kn[:, lanes], vals[:, lanes], None)
        dq_acc[:, lanes] = dq_part
        total[0, :, lanes] = dk_part.astype(F32)
        total[1, :, lanes] = dv_part.astype(F32)

    for side in (LEFT, RIGHT):

        @pl.when(exists[side])
        def _(side=side):
            halo_wait(side, 1)
            halo_wait(side, 0)

        for peer in range(cols):

            @pl.when(beyond[side][peer])
            def _(side=side, peer=peer):
                unit = unit_of(peer, owners[side])[0]
                far_pack[peer, 0] = pick_unit(unit, halo.at[side, 0])
                far_pack[peer, 1] = pick_unit(unit, halo.at[side, 1])
                far_copy(peer, owners[side]).start()

    for side in (LEFT, RIGHT, UP, DOWN):

        @pl.when(exists[side])
        def _(side=side):
            if side in (UP, DOWN):
                halo_wait(side, 1)
                halo_wait(side, 0)
            for head in range(heads):
                lanes = slice(head * hw, (head + 1) * hw)
                dq_part, dk_part, dv_part = attend(
                    head, halo[side, 0, :, lanes], halo[side, 1, :, lanes], None
                )
                dq_acc[:, lanes] += dq_part
                ret_out[side, 0, :, lanes] = dk_part
                ret_out[side, 1, :, lanes] = dv_part
            ret_copy(side).start()

    for peer in range(cols):

        @pl.when(is_far[peer])
        def _(peer=peer):
            far_wait(peer)

    mask = jnp.concatenate(
        [jnp.full((kb, tokens), used, jnp.int32) for used in mine_used], axis=0
    ) > 0
    for head in range(heads):
        lanes = slice(head * hw, (head + 1) * hw)
        dq_part, dk_part, dv_part = attend(
            head,
            far_in[:, 0, :, lanes].reshape(cols * kb, hw),
            far_in[:, 1, :, lanes].reshape(cols * kb, hw),
            mask,
        )
        dq_acc[:, lanes] += dq_part
        fret_out[:, 0, :, lanes] = dk_part.reshape(cols, kb, hw)
        fret_out[:, 1, :, lanes] = dv_part.reshape(cols, kb, hw)
    for peer in range(cols):

        @pl.when(is_far[peer])
        def _(peer=peer):
            fret_copy(peer).start()

    dq_norm = (dq_acc[...] * score_scale).astype(BF16).astype(F32)
    query_wide = q_raw[...].astype(F32)
    weighted = gain_q * dq_norm
    x_start(1, lane_columns([(0, row_sums(weighted * query_wide))])[0:8])
    q_factor = rates * rates * rates * x_finish(1) / full_width
    q_factor = to_columns(q_factor)[:, 0:1]
    dq_out[0, 0] = (q_rate * weighted - query_wide * q_factor).astype(BF16)

    for side in range(4):

        @pl.when(exists[side])
        def _(side=side):
            ret_wait(side)
            total[...] += ret_in[side].astype(F32)

    for peer in range(cols):

        @pl.when(is_far[peer])
        def _(peer=peer):
            fret_wait(peer)
            for unit in range(UNITS):
                picked = jnp.where(send_unit[peer] == unit, send_used[peer], 0)
                spread = jnp.full((kb, width), picked, jnp.int32) > 0
                place = slice(unit * kb, (unit + 1) * kb)
                for which in range(2):
                    total[which, place, :] += jnp.where(
                        spread, fret_in[peer, which].astype(F32), 0.0
                    )

    dk_norm = total[0].astype(BF16).astype(F32)
    key_wide = k_raw[...].astype(F32)
    weighted = gain_k * dk_norm
    x_start(2, lane_columns([(1, row_sums(weighted * key_wide))])[0:8])
    dv_out[0, 0] = total[1].astype(BF16)
    for side in range(4):

        @pl.when(exists[side])
        def _(side=side):
            halo_copy(side, 1, vals).wait_send()
            halo_copy(side, 0, kn).wait_send()
            ret_copy(side).wait_send()

    for peer in range(cols):

        @pl.when(is_far[peer])
        def _(peer=peer):
            fret_copy(peer).wait_send()

        for side in (LEFT, RIGHT):

            @pl.when(beyond[side][peer])
            def _(side=side, peer=peer):
                far_copy(peer, owners[side]).wait_send()

    k_factor = rates * rates * rates * x_finish(2) / full_width
    k_factor = to_columns(k_factor)[:, 1:2]
    dk_out[0, 0] = (k_rate * weighted - key_wide * k_factor).astype(BF16)


def copy_kernel(dq_in, dk_in, dv_in, dq_out, dk_out, dv_out, sem):
    pairs = ((dq_in, dq_out), (dk_in, dk_out), (dv_in, dv_out))
    copies = [
        pltpu.make_async_copy(source, target, sem.at[index])
        for index, (source, target) in enumerate(pairs)
    ]
    for copy in copies:
        copy.start()
    for copy in copies:
        copy.wait()


def body(sizes, q_raw, k_raw, values, upstream, outputs, logsumexp, gain_q, gain_k, far_list):
    rows, cols, parts = sizes
    tokens, width = q_raw.shape[2:]
    heads = logsumexp.shape[2]
    kb = tokens // UNITS
    delta_rows = -(-heads // 8) * 8
    shape = jax.ShapeDtypeStruct(q_raw.shape, BF16)
    vmem = pl.BlockSpec(memory_space=pltpu.VMEM)
    anywhere = pl.BlockSpec(memory_space=pltpu.HBM)
    tile = pltpu.VMEM((tokens, width), BF16)
    pair = (2, tokens, width)
    dma = pltpu.SemaphoreType.DMA
    grads = pl.pallas_call(
        functools.partial(kernel, sizes),
        out_shape=(pltpu.VMEM(q_raw.shape, BF16),) * 3,
        in_specs=[anywhere] * 5 + [vmem] * 3 + [pl.BlockSpec(memory_space=pltpu.SMEM)],
        out_specs=(vmem,) * 3,
        scratch_shapes=[
            tile,
            tile,
            tile,
            tile,
            tile,
            tile,
            tile,
            pltpu.VMEM((delta_rows, tokens), F32),
            pltpu.VMEM((tokens, width), F32),
            pltpu.VMEM((4,) + pair, BF16),
            pltpu.VMEM((cols, 2, kb, width), BF16),
            pltpu.VMEM((cols, 2, kb, width), BF16),
            pltpu.VMEM((4,) + pair, BF16),
            pltpu.VMEM((4,) + pair, BF16),
            pltpu.VMEM((cols, 2, kb, width), BF16),
            pltpu.VMEM((cols, 2, kb, width), BF16),
            pltpu.VMEM(pair, F32),
            pltpu.VMEM((3, parts, 8, 128), F32),
            dma((5,)),
            dma((4, 2)),
            dma((4, 2)),
            dma((cols,)),
            dma((cols,)),
            dma((4,)),
            dma((4,)),
            dma((cols,)),
            dma((cols,)),
            dma((3, parts)),
            dma((3, parts)),
        ],
        compiler_params=pltpu.CompilerParams(collective_id=0, has_side_effects=True),
    )(
        q_raw,
        k_raw,
        values,
        upstream,
        outputs,
        logsumexp.transpose(0, 2, 1, 3),
        gain_q,
        gain_k,
        far_list,
    )
    return pl.pallas_call(
        copy_kernel,
        out_shape=(shape, shape, shape),
        in_specs=[vmem] * 3,
        out_specs=(anywhere,) * 3,
        scratch_shapes=[dma((3,))],
        compiler_params=pltpu.CompilerParams(vmem_limit_bytes=4 << 20),
    )(*grads)


def solution(mesh):
    sizes = (mesh.shape["ha"], mesh.shape["wa"], mesh.shape["hd"])
    tile = P("ha", "wa", None, "hd")
    return jax.shard_map(
        functools.partial(body, sizes),
        mesh=mesh,
        in_specs=(tile,) * 5 + (P("ha", "wa", "hd", None), P("hd"), P("hd"), P("ha", None, None)),
        out_specs=(tile,) * 3,
        check_vma=False,
    )
```

```python
import functools
import math

import jax
import jax.numpy as jnp
from jax import lax
from jax.experimental import pallas as pl
from jax.experimental.pallas import tpu as pltpu
from jax.sharding import PartitionSpec as P

UNITS = 4
EPS = 1e-06
MESH = pl.DeviceIdType.MESH
LAST = (((1,), (1,)), ((), ()))
FIRST = (((0,), (0,)), ((), ()))
PLAIN = (((1,), (0,)), ((), ()))
UP, DOWN, LEFT, RIGHT = range(4)
F32 = jnp.float32
BF16 = jnp.bfloat16


def dot(a, b, dims):
    return lax.dot_general(a, b, dims, preferred_element_type=F32)


def kernel(
    sizes,
    q_hbm,
    k_hbm,
    v_hbm,
    u_hbm,
    o_hbm,
    lse_ref,
    gain_q_ref,
    gain_k_ref,
    far_ref,
    dq_out,
    dk_out,
    dv_out,
    q_raw,
    k_raw,
    vals,
    ups,
    outs,
    qn,
    kn,
    delta_ref,
    dq_acc,
    halo,
    far_pack,
    far_in,
    ret_out,
    ret_in,
    fret_out,
    fret_in,
    total,
    xbuf,
    load_sem,
    halo_send,
    halo_recv,
    far_send,
    far_recv,
    ret_send,
    ret_recv,
    fret_send,
    fret_recv,
    x_send,
    x_recv,
):
    rows, cols, parts = sizes
    row = lax.axis_index("ha")
    col = lax.axis_index("wa")
    me = lax.axis_index("hd")
    tokens, width = q_raw.shape
    heads = lse_ref.shape[1]
    hw = width // heads
    kb = tokens // UNITS
    full_width = width * parts
    slots = far_ref.shape[2]
    score_scale = 1.0 / math.sqrt(hw)

    loads = []
    for index, (source, target) in enumerate(
        ((v_hbm, vals), (k_hbm, k_raw), (q_hbm, q_raw), (u_hbm, ups), (o_hbm, outs))
    ):
        copy = pltpu.make_async_copy(source.at[0, 0], target, load_sem.at[index])
        copy.start()
        loads.append(copy)

    exists = (row > 0, row < rows - 1, col > 0, col < cols - 1)
    ids = ({"ha": row - 1}, {"ha": row + 1}, {"wa": col - 1}, {"wa": col + 1})
    is_far = [(col - peer) * (col - peer) >= 4 for peer in range(cols)]

    barrier = pltpu.get_barrier_semaphore()
    hd_ids = [{"hd": lax.rem(me + off, parts)} for off in range(1, parts)]
    for target in hd_ids:
        pl.semaphore_signal(barrier, inc=1, device_id=target, device_id_type=MESH)
    for side in range(4):

        @pl.when(exists[side])
        def _(side=side):
            pl.semaphore_signal(barrier, inc=1, device_id=ids[side], device_id_type=MESH)

    for peer in range(cols):

        @pl.when(is_far[peer])
        def _(peer=peer):
            pl.semaphore_signal(barrier, inc=1, device_id={"wa": peer}, device_id_type=MESH)

    def lane_columns(columns):
        lane = lax.broadcasted_iota(jnp.int32, (tokens, 128), 1)
        mat = jnp.zeros((tokens, 128), F32)
        for place, column in columns:
            mat = jnp.where(lane == place, column, mat)
        return mat.T

    def row_sums(block):
        acc = block[:, :hw]
        for head in range(1, heads):
            acc = acc + block[:, head * hw : (head + 1) * hw]
        return jnp.sum(acc, axis=1, keepdims=True)

    def to_columns(rows8):
        return jnp.concatenate([rows8] * (tokens // 8), axis=0).T

    def x_copy(which, off):
        return pltpu.make_async_remote_copy(
            src_ref=xbuf.at[which, me],
            dst_ref=xbuf.at[which, me],
            send_sem=x_send.at[which, off],
            recv_sem=x_recv.at[which, off],
            device_id=hd_ids[off - 1],
            device_id_type=MESH,
        )

    def x_start(which, rows8):
        xbuf[which, me] = rows8
        for off in range(1, parts):
            x_copy(which, off).start()

    def x_finish(which):
        for off in range(1, parts):
            x_copy(which, off).wait()
        acc = xbuf[which, 0]
        for part in range(1, parts):
            acc = acc + xbuf[which, part]
        return acc

    def halo_copy(side, which, source):
        return pltpu.make_async_remote_copy(
            src_ref=source,
            dst_ref=halo.at[side ^ 1, which],
            send_sem=halo_send.at[side, which],
            recv_sem=halo_recv.at[side ^ 1, which],
            device_id=ids[side],
            device_id_type=MESH,
        )

    def halo_wait(side, which):
        pltpu.make_async_remote_copy(
            src_ref=vals,
            dst_ref=halo.at[side, which],
            send_sem=halo_send.at[side, which],
            recv_sem=halo_recv.at[side, which],
            device_id=ids[side],
            device_id_type=MESH,
        ).wait_recv()

    def far_copy(peer):
        return pltpu.make_async_remote_copy(
            src_ref=far_pack.at[peer],
            dst_ref=far_in.at[col],
            send_sem=far_send.at[peer],
            recv_sem=far_recv.at[col],
            device_id={"wa": peer},
            device_id_type=MESH,
        )

    def far_wait(peer):
        pltpu.make_async_remote_copy(
            src_ref=far_pack.at[peer],
            dst_ref=far_in.at[peer],
            send_sem=far_send.at[peer],
            recv_sem=far_recv.at[peer],
            device_id={"wa": peer},
            device_id_type=MESH,
        ).wait_recv()

    def ret_copy(side):
        return pltpu.make_async_remote_copy(
            src_ref=ret_out.at[side],
            dst_ref=ret_in.at[side ^ 1],
            send_sem=ret_send.at[side],
            recv_sem=ret_recv.at[side ^ 1],
            device_id=ids[side],
            device_id_type=MESH,
        )

    def ret_wait(side):
        pltpu.make_async_remote_copy(
            src_ref=ret_out.at[side],
            dst_ref=ret_in.at[side],
            send_sem=ret_send.at[side],
            recv_sem=ret_recv.at[side],
            device_id=ids[side],
            device_id_type=MESH,
        ).wait_recv()

    def fret_copy(peer):
        return pltpu.make_async_remote_copy(
            src_ref=fret_out.at[peer],
            dst_ref=fret_in.at[col],
            send_sem=fret_send.at[peer],
            recv_sem=fret_recv.at[col],
            device_id={"wa": peer},
            device_id_type=MESH,
        )

    def fret_wait(peer):
        pltpu.make_async_remote_copy(
            src_ref=fret_out.at[peer],
            dst_ref=fret_in.at[peer],
            send_sem=fret_send.at[peer],
            recv_sem=fret_recv.at[peer],
            device_id={"wa": peer},
            device_id_type=MESH,
        ).wait_recv()

    pl.semaphore_wait(
        barrier,
        parts
        - 1
        + jnp.minimum(row, 1)
        + jnp.minimum(rows - 1 - row, 1)
        + (cols - 1),
    )
    for side in range(4):

        @pl.when(exists[side])
        def _(side=side):
            halo_copy(side, 1, v_hbm.at[0, 0]).start()

    loads[1].wait()
    key_wide = k_raw[...].astype(F32)
    key_squares = row_sums(key_wide * key_wide)
    loads[2].wait()
    query_wide = q_raw[...].astype(F32)
    query_squares = row_sums(query_wide * query_wide)
    sums = lane_columns([(0, query_squares), (1, key_squares)])[0:8]
    x_start(0, sums)

    loads[0].wait()
    loads[3].wait()
    loads[4].wait()
    delta_columns = []
    for head in range(heads):
        lanes = slice(head * hw, (head + 1) * hw)
        product = ups[:, lanes].astype(F32) * outs[:, lanes].astype(F32)
        delta_columns.append((head, jnp.sum(product, axis=1, keepdims=True)))
    delta_ref[...] = lane_columns(delta_columns)[0 : delta_ref.shape[0]]

    mine_used = []
    send_unit = []
    send_used = []
    for peer in range(cols):
        used = jnp.int32(0)
        unit = jnp.int32(0)
        asked = jnp.int32(0)
        for slot in range(slots):
            named = far_ref[0, col, slot] - peer * UNITS
            used = jnp.where((named >= 0) & (named < UNITS), 1, used)
            wanted = far_ref[0, peer, slot] - col * UNITS
            hit = (wanted >= 0) & (wanted < UNITS)
            unit = jnp.where(hit, wanted, unit)
            asked = jnp.where(hit, 1, asked)
        mine_used.append(used)
        send_unit.append(unit)
        send_used.append(asked)

    def pick_unit(peer, source):
        wanted = jnp.full((kb, width), send_unit[peer], jnp.int32)
        picked = source[0:kb, :].astype(F32)
        for unit in range(1, UNITS):
            block = source[unit * kb : (unit + 1) * kb, :].astype(F32)
            picked = jnp.where(wanted == unit, block, picked)
        return picked.astype(BF16)

    for peer in range(cols):

        @pl.when(is_far[peer])
        def _(peer=peer):
            far_pack[peer, 1] = pick_unit(peer, vals)

        @pl.when(jnp.logical_not(is_far[peer]))
        def _(peer=peer):
            far_in[peer] = jnp.zeros(far_in.shape[1:], BF16)

    gain_q = gain_q_ref[...].astype(F32).reshape(1, width)
    gain_k = gain_k_ref[...].astype(F32).reshape(1, width)
    rates = lax.rsqrt(x_finish(0) / full_width + EPS)
    rate_columns = to_columns(rates)
    q_rate = rate_columns[:, 0:1]
    k_rate = rate_columns[:, 1:2]
    kn[...] = (k_raw[...].astype(F32) * k_rate * gain_k).astype(BF16)
    for side in range(4):

        @pl.when(exists[side])
        def _(side=side):
            halo_copy(side, 0, kn).start()

    for peer in range(cols):

        @pl.when(is_far[peer])
        def _(peer=peer):
            far_pack[peer, 0] = pick_unit(peer, kn)
            far_copy(peer).start()

    qn[...] = (q_raw[...].astype(F32) * q_rate * gain_q).astype(BF16)

    def attend(head, key_head, value_head, mask):
        lanes = slice(head * hw, (head + 1) * hw)
        query_head = qn[:, lanes]
        upstream_head = ups[:, lanes]
        scores = dot(key_head, query_head, LAST) * score_scale
        weight = jnp.exp(scores - lse_ref[0, head])
        if mask is not None:
            weight = jnp.where(mask, weight, 0.0)
        dweight = dot(value_head, upstream_head, LAST)
        dscore = (weight * (dweight - delta_ref[head : head + 1, :])).astype(BF16)
        dq_part = dot(dscore, key_head, FIRST)
        dk_part = (dot(dscore, query_head, PLAIN) * score_scale).astype(BF16)
        dv_part = dot(weight.astype(BF16), upstream_head, PLAIN).astype(BF16)
        return dq_part, dk_part, dv_part

    for head in range(heads):
        lanes = slice(head * hw, (head + 1) * hw)
        dq_part, dk_part, dv_part = attend(head, kn[:, lanes], vals[:, lanes], None)
        dq_acc[:, lanes] = dq_part
        total[0, :, lanes] = dk_part.astype(F32)
        total[1, :, lanes] = dv_part.astype(F32)

    for side in (LEFT, RIGHT, UP, DOWN):

        @pl.when(exists[side])
        def _(side=side):
            halo_wait(side, 1)
            halo_wait(side, 0)
            for head in range(heads):
                lanes = slice(head * hw, (head + 1) * hw)
                dq_part, dk_part, dv_part = attend(
                    head, halo[side, 0, :, lanes], halo[side, 1, :, lanes], None
                )
                dq_acc[:, lanes] += dq_part
                ret_out[side, 0, :, lanes] = dk_part
                ret_out[side, 1, :, lanes] = dv_part
            ret_copy(side).start()

    for peer in range(cols):

        @pl.when(is_far[peer])
        def _(peer=peer):
            far_wait(peer)

    mask = jnp.concatenate(
        [jnp.full((kb, tokens), used, jnp.int32) for used in mine_used], axis=0
    ) > 0
    for head in range(heads):
        lanes = slice(head * hw, (head + 1) * hw)
        dq_part, dk_part, dv_part = attend(
            head,
            far_in[:, 0, :, lanes].reshape(cols * kb, hw),
            far_in[:, 1, :, lanes].reshape(cols * kb, hw),
            mask,
        )
        dq_acc[:, lanes] += dq_part
        fret_out[:, 0, :, lanes] = dk_part.reshape(cols, kb, hw)
        fret_out[:, 1, :, lanes] = dv_part.reshape(cols, kb, hw)
    for peer in range(cols):

        @pl.when(is_far[peer])
        def _(peer=peer):
            fret_copy(peer).start()

    dq_norm = (dq_acc[...] * score_scale).astype(BF16).astype(F32)
    query_wide = q_raw[...].astype(F32)
    weighted = gain_q * dq_norm
    x_start(1, lane_columns([(0, row_sums(weighted * query_wide))])[0:8])
    q_factor = rates * rates * rates * x_finish(1) / full_width
    q_factor = to_columns(q_factor)[:, 0:1]
    dq_out[0, 0] = (q_rate * weighted - query_wide * q_factor).astype(BF16)

    for side in range(4):

        @pl.when(exists[side])
        def _(side=side):
            ret_wait(side)
            total[...] += ret_in[side].astype(F32)

    for peer in range(cols):

        @pl.when(is_far[peer])
        def _(peer=peer):
            fret_wait(peer)
            for unit in range(UNITS):
                picked = jnp.where(send_unit[peer] == unit, send_used[peer], 0)
                spread = jnp.full((kb, width), picked, jnp.int32) > 0
                place = slice(unit * kb, (unit + 1) * kb)
                for which in range(2):
                    total[which, place, :] += jnp.where(
                        spread, fret_in[peer, which].astype(F32), 0.0
                    )

    dk_norm = total[0].astype(BF16).astype(F32)
    key_wide = k_raw[...].astype(F32)
    weighted = gain_k * dk_norm
    x_start(2, lane_columns([(1, row_sums(weighted * key_wide))])[0:8])
    dv_out[0, 0] = total[1].astype(BF16)
    for side in range(4):

        @pl.when(exists[side])
        def _(side=side):
            halo_copy(side, 1, v_hbm.at[0, 0]).wait_send()
            halo_copy(side, 0, kn).wait_send()
            ret_copy(side).wait_send()

    for peer in range(cols):

        @pl.when(is_far[peer])
        def _(peer=peer):
            far_copy(peer).wait_send()
            fret_copy(peer).wait_send()

    k_factor = rates * rates * rates * x_finish(2) / full_width
    k_factor = to_columns(k_factor)[:, 1:2]
    dk_out[0, 0] = (k_rate * weighted - key_wide * k_factor).astype(BF16)


def copy_kernel(dq_in, dk_in, dv_in, dq_out, dk_out, dv_out, sem):
    pairs = ((dq_in, dq_out), (dk_in, dk_out), (dv_in, dv_out))
    copies = [
        pltpu.make_async_copy(source, target, sem.at[index])
        for index, (source, target) in enumerate(pairs)
    ]
    for copy in copies:
        copy.start()
    for copy in copies:
        copy.wait()


def body(sizes, q_raw, k_raw, values, upstream, outputs, logsumexp, gain_q, gain_k, far_list):
    rows, cols, parts = sizes
    tokens, width = q_raw.shape[2:]
    heads = logsumexp.shape[2]
    kb = tokens // UNITS
    delta_rows = -(-heads // 8) * 8
    shape = jax.ShapeDtypeStruct(q_raw.shape, BF16)
    vmem = pl.BlockSpec(memory_space=pltpu.VMEM)
    anywhere = pl.BlockSpec(memory_space=pltpu.HBM)
    tile = pltpu.VMEM((tokens, width), BF16)
    pair = (2, tokens, width)
    dma = pltpu.SemaphoreType.DMA
    grads = pl.pallas_call(
        functools.partial(kernel, sizes),
        out_shape=(pltpu.VMEM(q_raw.shape, BF16),) * 3,
        in_specs=[anywhere] * 5 + [vmem] * 3 + [pl.BlockSpec(memory_space=pltpu.SMEM)],
        out_specs=(vmem,) * 3,
        scratch_shapes=[
            tile,
            tile,
            tile,
            tile,
            tile,
            tile,
            tile,
            pltpu.VMEM((delta_rows, tokens), F32),
            pltpu.VMEM((tokens, width), F32),
            pltpu.VMEM((4,) + pair, BF16),
            pltpu.VMEM((cols, 2, kb, width), BF16),
            pltpu.VMEM((cols, 2, kb, width), BF16),
            pltpu.VMEM((4,) + pair, BF16),
            pltpu.VMEM((4,) + pair, BF16),
            pltpu.VMEM((cols, 2, kb, width), BF16),
            pltpu.VMEM((cols, 2, kb, width), BF16),
            pltpu.VMEM(pair, F32),
            pltpu.VMEM((3, parts, 8, 128), F32),
            dma((5,)),
            dma((4, 2)),
            dma((4, 2)),
            dma((cols,)),
            dma((cols,)),
            dma((4,)),
            dma((4,)),
            dma((cols,)),
            dma((cols,)),
            dma((3, parts)),
            dma((3, parts)),
        ],
        compiler_params=pltpu.CompilerParams(collective_id=0, has_side_effects=True),
    )(
        q_raw,
        k_raw,
        values,
        upstream,
        outputs,
        logsumexp.transpose(0, 2, 1, 3),
        gain_q,
        gain_k,
        far_list,
    )
    return pl.pallas_call(
        copy_kernel,
        out_shape=(shape, shape, shape),
        in_specs=[vmem] * 3,
        out_specs=(anywhere,) * 3,
        scratch_shapes=[dma((3,))],
        compiler_params=pltpu.CompilerParams(vmem_limit_bytes=4 << 20),
    )(*grads)


def solution(mesh):
    sizes = (mesh.shape["ha"], mesh.shape["wa"], mesh.shape["hd"])
    tile = P("ha", "wa", None, "hd")
    return jax.shard_map(
        functools.partial(body, sizes),
        mesh=mesh,
        in_specs=(tile,) * 5 + (P("ha", "wa", "hd", None), P("hd"), P("hd"), P("ha", None, None)),
        out_specs=(tile,) * 3,
        check_vma=False,
    )
```
